768 devices in a mesh: blk: 16 (over y, core), cur: 48 (over x, z).
Axes of the slice: x: 4, y: 8, z: 12, core: 2. Of those that a mesh axis runs over, the one named last changes fastest.
Arguments:
- state: float32 [24576, 10240], P(('blk', 'cur')), may hold values from -6 to 6
- neighbour: int32 [24576, 4], P(('blk', 'cur')), may hold values from 0 to 24575, as said below
- neighbour_edge: int32 [24576, 4], P(('blk', 'cur')), may hold values from 0 to 3
- owner: int32 [24576, 1], P(('blk', 'cur')), may hold values from 0 to 47; in each aligned block of 32 rows (0 to 31, 32 to 63, ...) at most 2 rows name the same one
- surface: float32 [768, 384], P(('blk', 'cur')), may hold values from 0.5 to 1.5
- k_water: float32 [128, 128], replicated, may hold values from 0.002 to 0.2
- k_tracer: float32 [128, 128], replicated, may hold values from 0.002 to 0.2
Outputs:
- new_state: float32 [24576, 10240], P(('blk', 'cur'))
The draws below stay inside these ranges and needn't reach their ends.
Inputs may be any that keep to these rules, and one draw needn't show every extreme that they name: neighbour[e, k] = (e + s) mod 24576 with 1 <= |s| <= 32; for every element e with e % 32 == 0, edge 0 has s = -32, and for e % 32 == 31, edge 2 has s = 32. Among the elements of one device, no owner is named more than 2 times, a bound that some block reaches.
All inputs are finite; a program needn't handle non-finite values.
Results may differ from the reference program's by a relative error of at most 0.0003.
Values sent between devices are 32-bit elements; how exact they have to be, the bound alone decides.
A program may use at most 64 MiB of HBM per device.

```python
import math
import jax
import jax.numpy as jnp
import numpy as np
from jax import lax

ELEM_DEV = 32
GLL = 16
VARS = 5
LEV = 128
GPTS = 128
CAP = 2
ELEMS = 24576
N_CUR = 48
DEVICES = 768


def draw_neighbour(key, part):
    first_key = jax.random.fold_in(key, 11)
    second_key = jax.random.fold_in(key, 12)
    magnitude = jax.random.randint(first_key, (ELEMS, 4), 1, ELEM_DEV + 1)
    signs = jax.random.randint(second_key, (ELEMS, 4), 0, 2) * 2 - 1
    offsets = magnitude * signs
    positions = jnp.arange(ELEMS, dtype=jnp.int32)[:, None]
    column_ids = jnp.arange(4, dtype=jnp.int32)[None, :]
    offsets = jnp.where((positions % ELEM_DEV == 0) & (column_ids == 0), -ELEM_DEV, offsets)
    offsets = jnp.where((positions % ELEM_DEV == ELEM_DEV - 1) & (column_ids == 2), ELEM_DEV, offsets)
    return jnp.mod(positions + offsets, ELEMS).astype(jnp.int32)


def with_ends(entries, key, smallest, largest):
    dims = entries.shape
    index_at = [jax.random.randint(jax.random.fold_in(key, axis), (), 0, dims[axis]) for axis in range(len(dims))]
    entries = entries.at[tuple(index_at)].set(smallest)
    longest = dims.index(max(dims))
    index_at[longest] = (index_at[longest] + 1) % dims[longest]
    return entries.at[tuple(index_at)].set(largest)


def block_levels(own_key, shape, shards, smallest, top_value):
    loudness, own = 1.0, jax.random.fold_in(own_key, 6)
    for axis_at, shards_of in shards:
        steps = jnp.exp(jax.random.uniform(jax.random.fold_in(own, axis_at), (shards_of,), jnp.float32, smallest / len(shards), top_value / len(shards)))
        loudness = loudness * jnp.repeat(steps, shape[axis_at] // shards_of).reshape([-1 if axis == axis_at else 1 for axis in range(len(shape))])
    return loudness


def deal_out(rng, own, number, rows, number_of, top, most, skew):
    ranking = jax.random.permutation(rng, number_of)
    heavy_load, ordinary = shares(number_of, rows * top, most, skew, True), shares(number_of, rows * top, most, skew, False)
    places = jnp.arange(number_of)

    def named(tallies, turn):
        used = int((tallies > 0).sum())
        fixed = max(1, used // 4)
        shifted = fixed + (places - fixed + turn * (used - fixed)) % max(1, number_of - fixed)
        return jnp.zeros((number_of,), jnp.int32).at[ranking[jnp.where(places < fixed, places, shifted)]].set(jnp.asarray(tallies, jnp.int32))

    tallies = jnp.where(number % 4 == 0, named(heavy_load, number // 4), named(ordinary, number - number // 4 - 1))
    mixed = jax.random.permutation(jax.random.fold_in(own, 3), number_of)
    donor, taker = mixed[0:number_of // 2 * 2:2], mixed[1:number_of // 2 * 2:2]
    room = jnp.minimum(tallies[donor] - 1, most - tallies[taker]) // 2
    room = jnp.where((donor == ranking[0]) | (taker == ranking[0]) | (tallies[taker] == 0), 0, jnp.maximum(room, 0))
    shifted = jax.random.randint(jax.random.fold_in(own, 4), (number_of // 2,), 0, 1 << 20) % (room + 1)
    tallies = tallies.at[donor].add(-shifted).at[taker].add(shifted)
    items = jnp.searchsorted(jnp.cumsum(tallies), jnp.arange(rows * top), side="right").astype(jnp.int32)
    grid = items.reshape(top, rows).T
    grid = grid[jax.random.permutation(jax.random.fold_in(own, 1), rows)]
    turn = jax.random.randint(jax.random.fold_in(own, 2), (rows, 1), 0, top)
    return jnp.take_along_axis(grid, (jnp.arange(top)[None, :] + turn) % top, axis=1)


def shares(count, total, bound, skew, full):
    portions = [(1 << 20) // math.isqrt(grade ** skew) + 1 for grade in range(1, count + 1)]
    largest = bound if full else min(bound, max(-(-total // count), total * portions[0] // sum(portions)))
    least = 1 if total - largest >= count - 1 else 0
    given, surplus = [largest] + [least] * (count - 1), total - largest - least * (count - 1)
    while surplus > 0:
        movable = [i for i in range(1, count) if given[i] < largest] or [i for i in range(1, count) if given[i] < bound]
        pool, left = sum([portions[i] for i in movable]), surplus
        for i in movable:
            addition = min(bound - given[i], max(1, left * portions[i] // pool), surplus)
            given[i] = given[i] + addition
            surplus = surplus - addition
    return np.array(given)


def normal_values(own_key, shape, deviation, most, split=(), kind=jnp.bfloat16):
    factor_of = block_levels(own_key, shape, split, -0.22, 0.18) if split else 1.0
    values = jax.random.normal(own_key, shape, jnp.float32) * deviation * factor_of
    return jnp.minimum(jnp.maximum(values, -most), most).astype(kind)


def setup_inputs(seed: int = 0) -> dict:
    key_of = jax.random.split(jax.random.key(seed), 8)
    state = normal_values(key_of[0], (ELEMS, GLL * VARS * LEV), 1.0, 6.0, ((0, 768),), jnp.float32)
    neighbour = draw_neighbour(jax.random.fold_in(key_of[7], 71), 0)
    neighbour_edge = with_ends(jax.random.randint(key_of[2], (ELEMS, 4), 0, 4), jax.random.fold_in(key_of[2], 1), 0, 3).astype(jnp.int32)
    owner_keys = jax.random.split(jax.random.fold_in(key_of[3], 1), ELEMS // ELEM_DEV)
    owner_turns = jax.random.permutation(jax.random.fold_in(key_of[3], 3), ELEMS // ELEM_DEV)
    owner = jax.vmap(lambda own, number: deal_out(jax.random.fold_in(key_of[3], 2), own, number, ELEM_DEV, N_CUR, 1, CAP, 1))(owner_keys, owner_turns).reshape((ELEMS, 1))
    surface = jnp.clip(0.5 + 1.0 * jax.random.uniform(key_of[4], (DEVICES, N_CUR * CAP * 4), jnp.float32) ** block_levels(key_of[4], (DEVICES, N_CUR * CAP * 4), ((0, 768),), -0.2, 0.2), 0.5, 1.5)
    k_water = jnp.clip(jnp.exp(jax.random.uniform(key_of[5], (LEV, GPTS), jnp.float32, math.log(0.002), math.log(0.2))), 0.002, 0.2)
    k_tracer = jnp.clip(jnp.exp(jax.random.uniform(key_of[6], (LEV, GPTS), jnp.float32, math.log(0.002), math.log(0.2))), 0.002, 0.2)
    return dict(state=state, neighbour=neighbour, neighbour_edge=neighbour_edge, owner=owner, surface=surface, k_water=k_water, k_tracer=k_tracer)


HIGHEST = lax.Precision.HIGHEST

def gll_matrix():
    gll_nodes = np.array([-1.0, -1.0 / np.sqrt(5.0), 1.0 / np.sqrt(5.0), 1.0])
    weights = np.array([1.0 / np.prod([gll_nodes[col_at] - gll_nodes[other_at] for other_at in range(4) if other_at != col_at]) for col_at in range(4)])
    matrix = np.zeros((4, 4))
    for row_at in range(4):
        for col_at in range(4):
            if row_at != col_at:
                matrix[row_at, col_at] = weights[col_at] / weights[row_at] / (gll_nodes[row_at] - gll_nodes[col_at])
        matrix[row_at, row_at] = -np.sum(matrix[row_at])
    return matrix

def edge_table():
    return np.array([[0, 4, 8, 12], [12, 13, 14, 15], [15, 11, 7, 3], [3, 2, 1, 0]])

def column_tables():
    quad_weights = np.array([1.0 / 6.0, 5.0 / 6.0, 5.0 / 6.0, 1.0 / 6.0])
    project = np.zeros((4, 16))
    inject = np.zeros((16, 4))
    for row_at in range(4):
        for col_at in range(4):
            column_id = 2 * (row_at // 2) + col_at // 2
            project[column_id, 4 * row_at + col_at] = quad_weights[row_at] * quad_weights[col_at]
            inject[4 * row_at + col_at, column_id] = 1.0
    return (project, inject)

def tendency(state3):
    count = state3.shape[0]
    points_grid = state3.reshape(count, 4, 4, state3.shape[2], state3.shape[3])
    derivative = jnp.asarray(gll_matrix(), jnp.float32)
    along_x = jnp.einsum('ia,eajvl->eijvl', derivative, points_grid, precision=HIGHEST)
    along_y = jnp.einsum('jb,eibvl->eijvl', derivative, points_grid, precision=HIGHEST)
    east_wind = points_grid[:, :, :, 0:1, :]
    north_wind = points_grid[:, :, :, 1:2, :]
    result = -0.5 * (east_wind * along_x + north_wind * along_y)
    return result.reshape(state3.shape)

def edge_values(field):
    return jnp.take(field, jnp.asarray(edge_table().reshape(-1), jnp.int32), axis=1)

def pick_neighbours(edges_all, index_rows, edge_id):
    flat = edges_all.reshape(edges_all.shape[0] * 4, 4, edges_all.shape[2], edges_all.shape[3])
    picked = jnp.take(flat, (index_rows * 4 + edge_id).astype(jnp.int32), axis=0)
    return picked[:, :, ::-1]

def assemble(own_tend, picked):
    table = edge_table()
    onehot = (table[:, :, None] == np.arange(16)[None, None, :]).astype(np.float32)
    counts = 1.0 + onehot.sum(axis=(0, 1))
    gathered = jnp.einsum('ekp,xekvl->xpvl', jnp.asarray(onehot, jnp.float32), picked, precision=HIGHEST)
    return (own_tend + gathered) / jnp.asarray(counts, jnp.float32)[None, :, None, None]

def to_columns(state3):
    project, inject = column_tables()
    thermo = state3[:, :, 2:5, :]
    return jnp.einsum('cp,epvl->ecvl', jnp.asarray(project, jnp.float32), thermo, precision=HIGHEST)

def physics(columns, surface_values, k_water, k_tracer):
    temper = columns[:, 0, :]
    water = jax.nn.softplus(columns[:, 1, :])
    tracer = jax.nn.softplus(columns[:, 2, :])
    depth = water[:, :, None] * k_water[None] + tracer[:, :, None] * k_tracer[None]
    path_in = jnp.cumsum(depth, axis=1)
    path_out = path_in - depth
    path_all = path_in[:, -1:, :]
    downward = lax.optimization_barrier(jnp.mean(jnp.exp(-path_out) - jnp.exp(-path_in), axis=2))
    upward = lax.optimization_barrier(jnp.mean(jnp.exp(path_in - path_all) - jnp.exp(path_out - path_all), axis=2))
    emitted = lax.optimization_barrier(jnp.mean(1.0 - jnp.exp(-depth), axis=2))
    return 64.0 * downward + 2.0 * surface_values[:, None] * upward - 8.0 * jnp.tanh(temper) * emitted

def physics_blocks(columns, surface_values, k_water, k_tracer):
    column_count = columns.shape[0]
    block_size = 128 if column_count % 128 == 0 else column_count
    blocks = column_count // block_size
    col_blocks = columns.reshape(blocks, block_size, columns.shape[1], columns.shape[2])
    surf_blocks = surface_values.reshape(blocks, block_size)
    result = lax.map(lambda block_pair: physics(block_pair[0], block_pair[1], k_water, k_tracer), (col_blocks, surf_blocks))
    return result.reshape(column_count, columns.shape[2])

def slot_ranks(owner_id):
    count = owner_id.shape[0]
    same_owner = owner_id[:, None] == owner_id[None, :]
    earlier = jnp.arange(count)[None, :] < jnp.arange(count)[:, None]
    return lax.optimization_barrier(jnp.sum((same_owner & earlier).astype(jnp.int32), axis=1)).astype(jnp.int32)

def update(state3, dss, heating):
    project, inject = column_tables()
    at_points = jnp.einsum('pc,ecl->epl', jnp.asarray(inject, jnp.float32), heating, precision=HIGHEST)
    zeros_two = jnp.zeros((state3.shape[0], state3.shape[1], 2, state3.shape[3]), jnp.float32)
    physics_term = jnp.concatenate([zeros_two, at_points[:, :, None, :], zeros_two], axis=2)
    return state3 + 0.2 * (dss + physics_term)

def reference(state, neighbour, neighbour_edge, owner, surface, k_water, k_tracer):
    state3 = state.reshape(DEVICES, ELEM_DEV, GLL, VARS, LEV)
    tend_all = lax.map(tendency, state3)
    edges_all = edge_values(tend_all.reshape(ELEMS, GLL, VARS, LEV))
    owner_id = owner[:, 0].reshape(DEVICES, ELEM_DEV)
    slot_rank = jax.vmap(slot_ranks)(owner_id)
    device_ids = jnp.arange(DEVICES, dtype=jnp.int32)[:, None]
    phys_dev = (device_ids // N_CUR * N_CUR + owner_id).astype(jnp.int32)
    source = device_ids % N_CUR
    positions = ((source * CAP + slot_rank)[:, :, None] * 4 + jnp.arange(4, dtype=jnp.int32)[None, None, :]).astype(jnp.int32)
    surf_all = surface[phys_dev[:, :, None], positions]

    def per_device(inputs):
        state_blk, tend_blk, nbr_blk, edge_blk, surf_blk = inputs
        picked = pick_neighbours(edges_all, nbr_blk, edge_blk)
        dss = assemble(tend_blk, picked)
        heating = physics_blocks(to_columns(state_blk).reshape(ELEM_DEV * 4, 3, LEV), surf_blk.reshape(-1), k_water, k_tracer)
        return update(state_blk, dss, heating.reshape(ELEM_DEV, 4, LEV))
    result = lax.map(per_device, (state3, tend_all, neighbour.reshape(DEVICES, ELEM_DEV, 4), neighbour_edge.reshape(DEVICES, ELEM_DEV, 4), surf_all))
    return result.reshape(ELEMS, GLL * VARS * LEV)
```

```python
import functools
import math

import jax
import jax.numpy as jnp
import numpy as np
from jax import lax
from jax.experimental import pallas as pl
from jax.experimental.pallas import tpu as pltpu
from jax.sharding import PartitionSpec as P

MESH = pl.DeviceIdType.MESH
F32 = jnp.float32
BF16 = jnp.bfloat16
EDGES = ((0, 4, 8, 12), (12, 13, 14, 15), (15, 11, 7, 3), (3, 2, 1, 0))
RIM = (0, 1, 2, 3, 4, 7, 8, 11, 12, 13, 14, 15)
INNER = (5, 6, 9, 10)
SEND_ORDER = (0, 1, 3, 4, 2)
NE = 32
NV = 5
NL = 128


def gll_matrix():
    nodes = np.array([-1.0, -1.0 / np.sqrt(5.0), 1.0 / np.sqrt(5.0), 1.0])
    weights = np.array(
        [1.0 / np.prod([nodes[c] - nodes[o] for o in range(4) if o != c]) for c in range(4)]
    )
    matrix = np.zeros((4, 4))
    for r in range(4):
        for c in range(4):
            if r != c:
                matrix[r, c] = weights[c] / weights[r] / (nodes[r] - nodes[c])
        matrix[r, r] = -np.sum(matrix[r])
    return matrix


def weighted(terms):
    total = None
    for weight, value in terms:
        if abs(weight) < 1e-12:
            continue
        part = value * float(weight)
        total = part if total is None else total + part
    return total


def slab(p, v):
    return pl.ds((p * NV + v) * NL, NL)


def split(x):
    high = x.astype(BF16)
    low = (x - high.astype(F32)).astype(BF16)
    return high, low


def fold(x):
    rows = x.shape[0] // 8
    parts = [x[8 * i : 8 * i + 8] for i in range(rows)]
    while len(parts) > 1:
        parts = [parts[i] + parts[i + 1] for i in range(0, len(parts), 2)]
    return parts[0]


def kernel(
    nx,
    nz,
    state,
    nbr,
    nedge,
    owner,
    surface,
    kw,
    kt,
    out,
    own,
    left,
    right,
    inner,
    cols,
    wt,
    tran,
    st_part,
    sp_part,
    sq_part,
    shift,
    onehot,
    rhs,
    zbuf,
    xbuf,
    rim_send,
    rim_recv,
    z_send,
    z_recv,
    x_send,
    x_recv,
    copy_sem,
):
    blk = lax.axis_index("blk")
    cur = lax.axis_index("cur")
    n_blk = lax.axis_size("blk")
    n_cur = nx * nz
    n_dev = n_blk * n_cur
    me = blk * n_cur + cur
    my_x = cur // nz
    my_z = cur % nz

    def place(index):
        return (index // n_cur, index % n_cur)

    after = place(lax.rem(me + 1, n_dev))
    before = place(lax.rem(me + n_dev - 1, n_dev))

    def z_peer(j):
        return (blk, my_x * nz + lax.rem(my_z + j, nz))

    def x_peer(j):
        return (blk, lax.rem(my_x + j, nx) * nz + my_z)

    barrier = pltpu.get_barrier_semaphore()
    peers = [after, before] + [z_peer(j) for j in range(1, nz)] + [x_peer(j) for j in range(1, nx)]
    for peer in peers:
        pl.semaphore_signal(barrier, inc=1, device_id=peer, device_id_type=MESH)
    keep = pltpu.make_async_copy(surface, zbuf.at[my_z], copy_sem.at[0])
    keep.start()

    d_matrix = -0.5 * gll_matrix()

    def tend_rows(g, _):
        rows = pl.ds(pl.multiple_of(8 * g, 8), 8)
        wind_u = [state[rows, slab(p, 0)] for p in range(16)]
        wind_v = [state[rows, slab(p, 1)] for p in range(16)]
        for v in range(NV):
            q = [state[rows, slab(p, v)] for p in range(16)]
            for i in range(4):
                for j in range(4):
                    p = 4 * i + j
                    qx = weighted([(d_matrix[i, a], q[4 * a + j]) for a in range(4)])
                    qy = weighted([(d_matrix[j, b], q[4 * i + b]) for b in range(4)])
                    tend = wind_u[p] * qx + wind_v[p] * qy
                    if p in RIM:
                        own[v, RIM.index(p), rows, :] = tend
                    else:
                        inner[v, INNER.index(p), rows, :] = tend
        return 0

    lax.fori_loop(0, NE // 8, tend_rows, 0)

    quad = (1.0 / 6.0, 5.0 / 6.0, 5.0 / 6.0, 1.0 / 6.0)
    for c in range(4):
        points = [4 * i + j for i in range(4) for j in range(4) if 2 * (i // 2) + j // 2 == c]
        for r in range(3):
            value = weighted(
                [(quad[p // 4] * quad[p % 4], state[:, slab(p, 2 + r)]) for p in points]
            )
            if r > 0:
                value = jnp.maximum(value, 0.0) + jnp.log1p(jnp.exp(-jnp.abs(value)))
            cols[r, pl.ds(NE * c, NE), :] = value
    for r in range(2):
        turned = cols[r + 1].T
        high = turned.astype(BF16).astype(F32)
        wt[2 * r] = high
        wt[2 * r + 1] = turned - high

    pl.semaphore_wait(barrier, len(peers))
    rim_copies = {}
    for v in SEND_ORDER:
        for side, (dst, peer) in enumerate(((left, after), (right, before))):
            copy = pltpu.make_async_remote_copy(
                src_ref=own.at[v],
                dst_ref=dst.at[v],
                send_sem=rim_send.at[side, v],
                recv_sem=rim_recv.at[side, v],
                device_id=peer,
                device_id_type=MESH,
            )
            copy.start()
            rim_copies[side, v] = copy
    z_copies = []
    for j in range(1, nz):
        copy = pltpu.make_async_remote_copy(
            src_ref=surface,
            dst_ref=zbuf.at[my_z],
            send_sem=z_send.at[j - 1],
            recv_sem=z_recv.at[j - 1],
            device_id=z_peer(j),
            device_id_type=MESH,
        )
        copy.start()
        z_copies.append(copy)
    keep.wait()

    row_in_16 = lax.broadcasted_iota(jnp.int32, (128, NL), 0) % 16
    scale = -math.log2(math.e)

    def depth_group(group, _):
        rows = pl.ds(pl.multiple_of(16 * group, 16), 16)
        kw_f = kw[rows, :] * scale
        kt_f = kt[rows, :] * scale
        kw_h = kw_f.astype(BF16).astype(F32)
        kt_h = kt_f.astype(BF16).astype(F32)
        zero = jnp.zeros((32, NL), F32)
        k_stack = jnp.concatenate(
            [kw_h, kw_h, kw_f - kw_h, kt_h, kt_h, kt_f - kt_h, zero], axis=0
        )
        k_turned = k_stack.T.astype(BF16)
        w_h, w_l, t_h, t_l = (wt[i, rows, :] for i in range(4))
        w_stack = jnp.concatenate([w_h, w_l, w_h, t_h, t_l, t_h, zero], axis=0)
        for i in range(16):
            one = jnp.where(row_in_16 == i, w_stack, 0.0).astype(BF16)
            power = jnp.dot(k_turned, one, preferred_element_type=F32)
            passed = jnp.exp2(power)
            level = 16 * group + i
            tran[level] = passed
            st_part[pl.ds(pl.multiple_of(8 * level, 8), 8), :] = fold(passed)
        return 0

    lax.fori_loop(0, NL // 16, depth_group, 0)

    for copy in z_copies:
        copy.wait()
    x_copies = []
    keep_x = pltpu.make_async_copy(zbuf, xbuf.at[my_x], copy_sem.at[1])
    keep_x.start()
    for j in range(1, nx):
        copy = pltpu.make_async_remote_copy(
            src_ref=zbuf,
            dst_ref=xbuf.at[my_x],
            send_sem=x_send.at[j - 1],
            recv_sem=x_recv.at[j - 1],
            device_id=x_peer(j),
            device_id_type=MESH,
        )
        copy.start()
        x_copies.append(copy)

    def march(level, carry):
        down, up = carry
        back = NL - 1 - level
        down = down * tran[level]
        sp_part[pl.ds(pl.multiple_of(8 * level, 8), 8), :] = fold(down)
        sq_part[pl.ds(pl.multiple_of(8 * back, 8), 8), :] = fold(up)
        up = up * tran[back]
        return down, up

    ones = jnp.ones((NL, NL), F32)
    lax.fori_loop(0, NL, march, (ones, ones))

    def total(part):
        return sum(part[pl.ds(s, NL, stride=8), :] for s in range(8))

    sum_t, sum_p, sum_q = total(st_part), total(sp_part), total(sq_part)
    shift[0, pl.ds(0, 8), :] = jnp.full((8, NL), float(NL), F32)
    shift[0, pl.ds(8, NL), :] = sum_p
    shift[1, pl.ds(0, 8), :] = jnp.broadcast_to(sum_p[NL - 1 : NL], (8, NL))
    shift[1, pl.ds(8, NL), :] = sum_q
    inv = 1.0 / NL
    downward = ((shift[0, pl.ds(7, NL), :] - sum_p) * (64.0 * inv)).T
    upward = ((sum_q - shift[1, pl.ds(7, NL), :]) * (2.0 * inv)).T
    emitted = (8.0 - sum_t * (8.0 * inv)).T

    base = me * NE - NE
    elems = n_dev * NE
    local = nbr[...] - base
    local = jnp.where(local < 0, local + elems, local)
    local = jnp.where(local >= elems, local - elems, local)
    target = nedge[...] * 192 + local
    lane = lax.broadcasted_iota(jnp.int32, (NE, 768), 1)
    for k in range(4):
        want = target[:, k : k + 1]
        hit = (lane == want) | (lane == want + 96)
        onehot[pl.ds(NE * k, NE), :] = hit.astype(F32).astype(BF16)

    own_col = owner[...].astype(F32)
    sub = lax.broadcasted_iota(jnp.int32, (NE, NL), 0)
    lan = lax.broadcasted_iota(jnp.int32, (NE, NL), 1)
    wide = jnp.broadcast_to(own_col, (NE, NL))
    own_row = jnp.sum(jnp.where(sub == lan, wide, 0.0), axis=0, keepdims=True)
    earlier = (wide == own_row) & (lan < sub)
    rank = jnp.sum(jnp.where(earlier, 1.0, 0.0), axis=1, keepdims=True).astype(jnp.int32)

    keep_x.wait()
    for copy in x_copies:
        copy.wait()
    width = surface.shape[1]
    owner_wide = jnp.broadcast_to(owner[...], (NE, width))
    picked = jnp.zeros((NE, width), F32)
    for x in range(nx):
        for z in range(nz):
            row = jnp.broadcast_to(xbuf[x, z], (NE, width))
            picked = jnp.where(owner_wide == x * nz + z, row, picked)
    s_lane = lax.broadcasted_iota(jnp.int32, (NE, width), 1)
    first = (cur * (width // (4 * n_cur)) + rank) * 4
    heat = []
    for c in range(4):
        surf = jnp.sum(jnp.where(s_lane == first + c, picked, 0.0), axis=1, keepdims=True)
        part = slice(NE * c, NE * c + NE)
        heat.append(
            0.2
            * (
                downward[part]
                + surf * upward[part]
                - jnp.tanh(cols[0, pl.ds(NE * c, NE), :]) * emitted[part]
            )
        )

    count = [1 + sum(p in edge for edge in EDGES) for p in range(16)]
    for v in SEND_ORDER:
        rim_copies[0, v].wait()
        rim_copies[1, v].wait()
        for f in range(4):
            for m in range(4):
                b = RIM.index(EDGES[f][3 - m])
                lanes = pl.ds(NL * m, NL)
                for s, ref in enumerate((left, own, right)):
                    high, low = split(ref[v, b])
                    rhs[pl.ds(192 * f + 32 * s, 32), lanes] = high
                    rhs[pl.ds(192 * f + 96 + 32 * s, 32), lanes] = low
        got = jnp.dot(onehot[...], rhs[...], preferred_element_type=F32)
        for p in range(16):
            if p in RIM:
                tend = own[v, RIM.index(p)]
            else:
                tend = inner[v, INNER.index(p)]
            for k in range(4):
                if p in EDGES[k]:
                    m = EDGES[k].index(p)
                    tend = tend + got[NE * k : NE * k + NE, NL * m : NL * m + NL]
            value = state[:, slab(p, v)] + tend * (0.2 / count[p])
            if v == 2:
                value = value + heat[2 * (p // 8) + (p % 4) // 2]
            out[:, slab(p, v)] = value


def per_device(nx, nz, state, neighbour, neighbour_edge, owner, surface, k_water, k_tracer):
    width = surface.shape[1]
    vmem = pl.BlockSpec(memory_space=pltpu.VMEM)
    sem = pltpu.SemaphoreType.DMA
    return pl.pallas_call(
        functools.partial(kernel, nx, nz),
        out_shape=jax.ShapeDtypeStruct(state.shape, F32),
        in_specs=[vmem] * 7,
        out_specs=vmem,
        scratch_shapes=[
            pltpu.VMEM((NV, 12, NE, NL), F32),
            pltpu.VMEM((NV, 12, NE, NL), F32),
            pltpu.VMEM((NV, 12, NE, NL), F32),
            pltpu.VMEM((NV, 4, NE, NL), F32),
            pltpu.VMEM((3, NL, NL), F32),
            pltpu.VMEM((4, NL, NL), F32),
            pltpu.VMEM((NL, NL, NL), F32),
            pltpu.VMEM((8 * NL, NL), F32),
            pltpu.VMEM((8 * NL, NL), F32),
            pltpu.VMEM((8 * NL, NL), F32),
            pltpu.VMEM((2, NL + 8, NL), F32),
            pltpu.VMEM((NL, 768), BF16),
            pltpu.VMEM((768, 512), BF16),
            pltpu.VMEM((nz, 1, width), F32),
            pltpu.VMEM((nx, nz, 1, width), F32),
            sem((2, NV)),
            sem((2, NV)),
            sem((max(nz - 1, 1),)),
            sem((max(nz - 1, 1),)),
            sem((max(nx - 1, 1),)),
            sem((max(nx - 1, 1),)),
            sem((2,)),
        ],
        compiler_params=pltpu.CompilerParams(collective_id=0, has_side_effects=True),
        name="dynamics_physics",
    )(state, neighbour, neighbour_edge, owner, surface, k_water, k_tracer)


def solution(mesh):
    n_cur = mesh.shape["cur"]
    nx = 4 if n_cur % 4 == 0 and n_cur > 4 else 2
    nz = n_cur // nx
    both = P(("blk", "cur"), None)
    return jax.shard_map(
        functools.partial(per_device, nx, nz),
        mesh=mesh,
        in_specs=(both, both, both, both, both, P(), P()),
        out_specs=both,
        check_vma=False,
    )
```

```python
import functools
import math

import jax
import jax.numpy as jnp
import numpy as np
from jax import lax
from jax.experimental import pallas as pl
from jax.experimental.pallas import tpu as pltpu
from jax.sharding import PartitionSpec as P

MESH = pl.DeviceIdType.MESH
F32 = jnp.float32
BF16 = jnp.bfloat16
EDGES = ((0, 4, 8, 12), (12, 13, 14, 15), (15, 11, 7, 3), (3, 2, 1, 0))
RIM = (0, 1, 2, 3, 4, 7, 8, 11, 12, 13, 14, 15)
INNER = (5, 6, 9, 10)
SEND_ORDER = (0, 1, 3, 4, 2)
NE = 32
NV = 5
NL = 128


def gll_matrix():
    nodes = np.array([-1.0, -1.0 / np.sqrt(5.0), 1.0 / np.sqrt(5.0), 1.0])
    weights = np.array(
        [1.0 / np.prod([nodes[c] - nodes[o] for o in range(4) if o != c]) for c in range(4)]
    )
    matrix = np.zeros((4, 4))
    for r in range(4):
        for c in range(4):
            if r != c:
                matrix[r, c] = weights[c] / weights[r] / (nodes[r] - nodes[c])
        matrix[r, r] = -np.sum(matrix[r])
    return matrix


def weighted(terms):
    total = None
    for weight, value in terms:
        if abs(weight) < 1e-12:
            continue
        part = value * float(weight)
        total = part if total is None else total + part
    return total


def slab(p, v):
    return pl.ds((p * NV + v) * NL, NL)


def split(x):
    high = x.astype(BF16)
    low = (x - high.astype(F32)).astype(BF16)
    return high, low


def fold(x):
    rows = x.shape[0] // 8
    parts = [x[8 * i : 8 * i + 8] for i in range(rows)]
    while len(parts) > 1:
        parts = [parts[i] + parts[i + 1] for i in range(0, len(parts), 2)]
    return parts[0]


def kernel(
    nx,
    nz,
    state,
    nbr,
    nedge,
    owner,
    surface,
    kw,
    kt,
    out,
    own,
    left,
    right,
    inner,
    cols,
    wt,
    tran,
    st_part,
    sp_part,
    sq_part,
    shift,
    onehot,
    rhs,
    zbuf,
    xbuf,
    rim_send,
    rim_recv,
    z_send,
    z_recv,
    x_send,
    x_recv,
    copy_sem,
):
    blk = lax.axis_index("blk")
    cur = lax.axis_index("cur")
    n_blk = lax.axis_size("blk")
    n_cur = nx * nz
    n_dev = n_blk * n_cur
    me = blk * n_cur + cur
    my_x = cur // nz
    my_z = cur % nz

    def place(index):
        return (index // n_cur, index % n_cur)

    after = place(lax.rem(me + 1, n_dev))
    before = place(lax.rem(me + n_dev - 1, n_dev))

    def z_peer(j):
        return (blk, my_x * nz + lax.rem(my_z + j, nz))

    def x_peer(j):
        return (blk, lax.rem(my_x + j, nx) * nz + my_z)

    barrier = pltpu.get_barrier_semaphore()
    peers = [after, before] + [z_peer(j) for j in range(1, nz)] + [x_peer(j) for j in range(1, nx)]
    for peer in peers:
        pl.semaphore_signal(barrier, inc=1, device_id=peer, device_id_type=MESH)
    keep = pltpu.make_async_copy(surface, zbuf.at[my_z], copy_sem.at[0])
    keep.start()

    d_matrix = -0.5 * gll_matrix()

    def tend_rows(v, g, _):
        rows = pl.ds(pl.multiple_of(8 * g, 8), 8)
        q = [state[rows, slab(p, v)] for p in range(16)]
        for i in range(4):
            for j in range(4):
                p = 4 * i + j
                qx = weighted([(d_matrix[i, a], q[4 * a + j]) for a in range(4)])
                qy = weighted([(d_matrix[j, b], q[4 * i + b]) for b in range(4)])
                tend = state[rows, slab(p, 0)] * qx + state[rows, slab(p, 1)] * qy
                if p in RIM:
                    own[v, RIM.index(p), rows, :] = tend
                else:
                    inner[v, INNER.index(p), rows, :] = tend
        return 0

    lax.fori_loop(0, NE // 8, functools.partial(tend_rows, SEND_ORDER[0]), 0)
    pl.semaphore_wait(barrier, len(peers))
    z_copies = []
    for j in range(1, nz):
        copy = pltpu.make_async_remote_copy(
            src_ref=surface,
            dst_ref=zbuf.at[my_z],
            send_sem=z_send.at[j - 1],
            recv_sem=z_recv.at[j - 1],
            device_id=z_peer(j),
            device_id_type=MESH,
        )
        copy.start()
        z_copies.append(copy)
    rim_copies = {}
    for v in SEND_ORDER:
        if v != SEND_ORDER[0]:
            lax.fori_loop(0, NE // 8, functools.partial(tend_rows, v), 0)
        for side, (dst, peer) in enumerate(((left, after), (right, before))):
            copy = pltpu.make_async_remote_copy(
                src_ref=own.at[v],
                dst_ref=dst.at[v],
                send_sem=rim_send.at[side, v],
                recv_sem=rim_recv.at[side, v],
                device_id=peer,
                device_id_type=MESH,
            )
            copy.start()
            rim_copies[side, v] = copy

    quad = (1.0 / 6.0, 5.0 / 6.0, 5.0 / 6.0, 1.0 / 6.0)
    for c in range(4):
        points = [4 * i + j for i in range(4) for j in range(4) if 2 * (i // 2) + j // 2 == c]
        for r in range(3):
            value = weighted(
                [(quad[p // 4] * quad[p % 4], state[:, slab(p, 2 + r)]) for p in points]
            )
            if r > 0:
                value = jnp.maximum(value, 0.0) + jnp.log1p(jnp.exp(-jnp.abs(value)))
            cols[r, pl.ds(NE * c, NE), :] = value
    for r in range(2):
        turned = cols[r + 1].T
        high = turned.astype(BF16).astype(F32)
        wt[2 * r] = high
        wt[2 * r + 1] = turned - high

    keep.wait()

    row_in_16 = lax.broadcasted_iota(jnp.int32, (128, NL), 0) % 16
    scale = -math.log2(math.e)

    def depth_group(group, _):
        rows = pl.ds(pl.multiple_of(16 * group, 16), 16)
        kw_f = kw[rows, :] * scale
        kt_f = kt[rows, :] * scale
        kw_h = kw_f.astype(BF16).astype(F32)
        kt_h = kt_f.astype(BF16).astype(F32)
        zero = jnp.zeros((32, NL), F32)
        k_stack = jnp.concatenate(
            [kw_h, kw_h, kw_f - kw_h, kt_h, kt_h, kt_f - kt_h, zero], axis=0
        )
        k_turned = k_stack.T.astype(BF16)
        w_h, w_l, t_h, t_l = (wt[i, rows, :] for i in range(4))
        w_stack = jnp.concatenate([w_h, w_l, w_h, t_h, t_l, t_h, zero], axis=0)
        for i in range(16):
            one = jnp.where(row_in_16 == i, w_stack, 0.0).astype(BF16)
            power = jnp.dot(k_turned, one, preferred_element_type=F32)
            passed = jnp.exp2(power)
            level = 16 * group + i
            tran[level] = passed
            st_part[pl.ds(pl.multiple_of(8 * level, 8), 8), :] = fold(passed)
        return 0

    lax.fori_loop(0, NL // 16, depth_group, 0)

    for copy in z_copies:
        copy.wait()
    x_copies = []
    keep_x = pltpu.make_async_copy(zbuf, xbuf.at[my_x], copy_sem.at[1])
    keep_x.start()
    for j in range(1, nx):
        copy = pltpu.make_async_remote_copy(
            src_ref=zbuf,
            dst_ref=xbuf.at[my_x],
            send_sem=x_send.at[j - 1],
            recv_sem=x_recv.at[j - 1],
            device_id=x_peer(j),
            device_id_type=MESH,
        )
        copy.start()
        x_copies.append(copy)

    def march(level, carry):
        down, up = carry
        back = NL - 1 - level
        down = down * tran[level]
        sp_part[pl.ds(pl.multiple_of(8 * level, 8), 8), :] = fold(down)
        sq_part[pl.ds(pl.multiple_of(8 * back, 8), 8), :] = fold(up)
        up = up * tran[back]
        return down, up

    ones = jnp.ones((NL, NL), F32)
    lax.fori_loop(0, NL, march, (ones, ones))

    def total(part):
        return sum(part[pl.ds(s, NL, stride=8), :] for s in range(8))

    sum_t, sum_p, sum_q = total(st_part), total(sp_part), total(sq_part)
    shift[0, pl.ds(0, 8), :] = jnp.full((8, NL), float(NL), F32)
    shift[0, pl.ds(8, NL), :] = sum_p
    shift[1, pl.ds(0, 8), :] = jnp.broadcast_to(sum_p[NL - 1 : NL], (8, NL))
    shift[1, pl.ds(8, NL), :] = sum_q
    inv = 1.0 / NL
    downward = ((shift[0, pl.ds(7, NL), :] - sum_p) * (64.0 * inv)).T
    upward = ((sum_q - shift[1, pl.ds(7, NL), :]) * (2.0 * inv)).T
    emitted = (8.0 - sum_t * (8.0 * inv)).T

    base = me * NE - NE
    elems = n_dev * NE
    local = nbr[...] - base
    local = jnp.where(local < 0, local + elems, local)
    local = jnp.where(local >= elems, local - elems, local)
    target = nedge[...] * 192 + local
    lane = lax.broadcasted_iota(jnp.int32, (NE, 768), 1)
    sub = lax.broadcasted_iota(jnp.int32, (NE, NE), 0)
    lan = lax.broadcasted_iota(jnp.int32, (NE, NE), 1)

    def column(row):
        return jnp.sum(jnp.where(sub == lan, row, 0.0), axis=1, keepdims=True)

    for k in range(4):
        row = jnp.broadcast_to(target[k : k + 1, :].astype(F32), (NE, NE))
        want = column(row).astype(jnp.int32)
        hit = (lane == want) | (lane == want + 96)
        onehot[pl.ds(NE * k, NE), :] = hit.astype(F32).astype(BF16)

    own_row = jnp.broadcast_to(owner[...].astype(F32), (NE, NE))
    own_col = column(own_row)
    earlier = (own_col == own_row) & (lan < sub)
    rank = jnp.sum(jnp.where(earlier, 1.0, 0.0), axis=1, keepdims=True).astype(jnp.int32)

    keep_x.wait()
    for copy in x_copies:
        copy.wait()
    width = surface.shape[1]
    owner_wide = jnp.broadcast_to(own_col.astype(jnp.int32), (NE, width))
    picked = jnp.zeros((NE, width), F32)
    for x in range(nx):
        for z in range(nz):
            row = jnp.broadcast_to(xbuf[x, z], (NE, width))
            picked = jnp.where(owner_wide == x * nz + z, row, picked)
    s_lane = lax.broadcasted_iota(jnp.int32, (NE, width), 1)
    first = (cur * (width // (4 * n_cur)) + rank) * 4
    heat = []
    for c in range(4):
        surf = jnp.sum(jnp.where(s_lane == first + c, picked, 0.0), axis=1, keepdims=True)
        part = slice(NE * c, NE * c + NE)
        heat.append(
            0.2
            * (
                downward[part]
                + surf * upward[part]
                - jnp.tanh(cols[0, pl.ds(NE * c, NE), :]) * emitted[part]
            )
        )

    count = [1 + sum(p in edge for edge in EDGES) for p in range(16)]
    for v in SEND_ORDER:
        rim_copies[0, v].wait()
        rim_copies[1, v].wait()
        for f in range(4):
            for m in range(4):
                b = RIM.index(EDGES[f][3 - m])
                lanes = pl.ds(NL * m, NL)
                for s, ref in enumerate((left, own, right)):
                    high, low = split(ref[v, b])
                    rhs[pl.ds(192 * f + 32 * s, 32), lanes] = high
                    rhs[pl.ds(192 * f + 96 + 32 * s, 32), lanes] = low
        got = jnp.dot(onehot[...], rhs[...], preferred_element_type=F32)
        for p in range(16):
            if p in RIM:
                tend = own[v, RIM.index(p)]
            else:
                tend = inner[v, INNER.index(p)]
            for k in range(4):
                if p in EDGES[k]:
                    m = EDGES[k].index(p)
                    tend = tend + got[NE * k : NE * k + NE, NL * m : NL * m + NL]
            value = state[:, slab(p, v)] + tend * (0.2 / count[p])
            if v == 2:
                value = value + heat[2 * (p // 8) + (p % 4) // 2]
            out[:, slab(p, v)] = value


def per_device(nx, nz, state, neighbour, neighbour_edge, owner, surface, k_water, k_tracer):
    width = surface.shape[1]
    vmem = pl.BlockSpec(memory_space=pltpu.VMEM)
    sem = pltpu.SemaphoreType.DMA
    return pl.pallas_call(
        functools.partial(kernel, nx, nz),
        out_shape=pltpu.VMEM(state.shape, F32),
        in_specs=[vmem] * 7,
        out_specs=vmem,
        scratch_shapes=[
            pltpu.VMEM((NV, 12, NE, NL), F32),
            pltpu.VMEM((NV, 12, NE, NL), F32),
            pltpu.VMEM((NV, 12, NE, NL), F32),
            pltpu.VMEM((NV, 4, NE, NL), F32),
            pltpu.VMEM((3, NL, NL), F32),
            pltpu.VMEM((4, NL, NL), F32),
            pltpu.VMEM((NL, NL, NL), F32),
            pltpu.VMEM((8 * NL, NL), F32),
            pltpu.VMEM((8 * NL, NL), F32),
            pltpu.VMEM((8 * NL, NL), F32),
            pltpu.VMEM((2, NL + 8, NL), F32),
            pltpu.VMEM((NL, 768), BF16),
            pltpu.VMEM((768, 512), BF16),
            pltpu.VMEM((nz, 1, width), F32),
            pltpu.VMEM((nx, nz, 1, width), F32),
            sem((2, NV)),
            sem((2, NV)),
            sem((max(nz - 1, 1),)),
            sem((max(nz - 1, 1),)),
            sem((max(nx - 1, 1),)),
            sem((max(nx - 1, 1),)),
            sem((2,)),
        ],
        compiler_params=pltpu.CompilerParams(collective_id=0, has_side_effects=True),
        name="dynamics_physics",
    )(state, neighbour.T, neighbour_edge.T, owner.T, surface, k_water, k_tracer)


def solution(mesh):
    n_cur = mesh.shape["cur"]
    nx = 4 if n_cur % 4 == 0 and n_cur > 4 else 2
    nz = n_cur // nx
    both = P(("blk", "cur"), None)
    return jax.shard_map(
        functools.partial(per_device, nx, nz),
        mesh=mesh,
        in_specs=(both, both, both, both, both, P(), P()),
        out_specs=both,
        check_vma=False,
    )
```

```python
import functools
import math

import jax
import jax.numpy as jnp
import numpy as np
from jax import lax
from jax.experimental import pallas as pl
from jax.experimental.pallas import tpu as pltpu
from jax.sharding import PartitionSpec as P

MESH = pl.DeviceIdType.MESH
F32 = jnp.float32
BF16 = jnp.bfloat16
EDGES = ((0, 4, 8, 12), (12, 13, 14, 15), (15, 11, 7, 3), (3, 2, 1, 0))
RIM = (0, 1, 2, 3, 4, 7, 8, 11, 12, 13, 14, 15)
INNER = (5, 6, 9, 10)
SEND_ORDER = (0, 1, 3, 4, 2)
NE = 32
NV = 5
NL = 128


def gll_matrix():
    nodes = np.array([-1.0, -1.0 / np.sqrt(5.0), 1.0 / np.sqrt(5.0), 1.0])
    weights = np.array(
        [1.0 / np.prod([nodes[c] - nodes[o] for o in range(4) if o != c]) for c in range(4)]
    )
    matrix = np.zeros((4, 4))
    for r in range(4):
        for c in range(4):
            if r != c:
                matrix[r, c] = weights[c] / weights[r] / (nodes[r] - nodes[c])
        matrix[r, r] = -np.sum(matrix[r])
    return matrix


def weighted(terms):
    total = None
    for weight, value in terms:
        if abs(weight) < 1e-12:
            continue
        part = value * float(weight)
        total = part if total is None else total + part
    return total


def slab(p, v):
    return pl.ds((p * NV + v) * NL, NL)


def split(x):
    high = x.astype(BF16)
    low = (x - high.astype(F32)).astype(BF16)
    return high, low


def fold(x):
    rows = x.shape[0] // 8
    parts = [x[8 * i : 8 * i + 8] for i in range(rows)]
    while len(parts) > 1:
        parts = [parts[i] + parts[i + 1] for i in range(0, len(parts), 2)]
    return parts[0]


def kernel(
    nx,
    nz,
    state_in,
    nbr_in,
    nedge_in,
    owner_in,
    surface_in,
    kw_in,
    kt_in,
    out,
    state,
    nbr,
    nedge,
    owner,
    surface,
    kw,
    kt,
    own,
    left,
    right,
    inner,
    cols,
    wt,
    tran,
    st_part,
    sp_part,
    sq_part,
    shift,
    onehot,
    rhs,
    zbuf,
    xbuf,
    rim_send,
    rim_recv,
    z_send,
    z_recv,
    x_send,
    x_recv,
    copy_sem,
    load_sem,
    z_near,
    z_mid,
    z_far,
    x_near,
):
    blk = lax.axis_index("blk")
    cur = lax.axis_index("cur")
    n_blk = lax.axis_size("blk")
    n_cur = nx * nz
    n_dev = n_blk * n_cur
    me = blk * n_cur + cur
    my_x = cur // nz
    my_z = cur % nz

    def place(index):
        return (index // n_cur, index % n_cur)

    after = place(lax.rem(me + 1, n_dev))
    before = place(lax.rem(me + n_dev - 1, n_dev))

    def z_peer(j):
        return (blk, my_x * nz + lax.rem(my_z + j + nz, nz))

    def x_peer(j):
        return (blk, lax.rem(my_x + j + nx, nx) * nz + my_z)

    def tell(sem, peer):
        pl.semaphore_signal(sem, inc=1, device_id=peer, device_id_type=MESH)

    barrier = pltpu.get_barrier_semaphore()
    peers = [after, before, z_peer(1), z_peer(-1), x_peer(1), x_peer(-1)]
    for peer in peers:
        tell(barrier, peer)
    loads = []
    pairs = (
        (state_in, state),
        (surface_in, surface),
        (kw_in, kw),
        (kt_in, kt),
        (nbr_in, nbr),
        (nedge_in, nedge),
        (owner_in, owner),
    )
    for i, (src, dst) in enumerate(pairs):
        load = pltpu.make_async_copy(src, dst, load_sem.at[i])
        load.start()
        loads.append(load)
    loads[0].wait()

    d_matrix = -0.5 * gll_matrix()

    def tend_rows(v, g, _):
        rows = pl.ds(pl.multiple_of(8 * g, 8), 8)
        q = [state[rows, slab(p, v)] for p in range(16)]
        for i in range(4):
            for j in range(4):
                p = 4 * i + j
                qx = weighted([(d_matrix[i, a], q[4 * a + j]) for a in range(4)])
                qy = weighted([(d_matrix[j, b], q[4 * i + b]) for b in range(4)])
                tend = state[rows, slab(p, 0)] * qx + state[rows, slab(p, 1)] * qy
                if p in RIM:
                    own[v, RIM.index(p), rows, :] = tend
                else:
                    inner[v, INNER.index(p), rows, :] = tend
        return 0

    def tend_of(v):
        lax.fori_loop(0, NE // 8, functools.partial(tend_rows, v), 0)

    rim_copies = {}

    def send_rim(v):
        for side, (dst, peer) in enumerate(((left, after), (right, before))):
            copy = pltpu.make_async_remote_copy(
                src_ref=own.at[v],
                dst_ref=dst.at[v],
                send_sem=rim_send.at[side, v],
                recv_sem=rim_recv.at[side, v],
                device_id=peer,
                device_id_type=MESH,
            )
            copy.start()
            rim_copies[side, v] = copy

    tend_of(SEND_ORDER[0])
    pl.semaphore_wait(barrier, len(peers))
    tell(z_near, z_peer(1))
    tell(z_near, z_peer(-1))
    tell(x_near, x_peer(1))
    tell(x_near, x_peer(-1))
    send_rim(SEND_ORDER[0])
    tend_of(SEND_ORDER[1])
    send_rim(SEND_ORDER[1])
    for load in loads[1:]:
        load.wait()
    keep = pltpu.make_async_copy(surface, zbuf.at[my_z], copy_sem.at[0])
    keep.start()
    pl.semaphore_wait(z_near, 2)
    tell(z_mid, z_peer(2))
    tell(z_mid, z_peer(-2))
    for v in SEND_ORDER[2:]:
        tend_of(v)

    quad = (1.0 / 6.0, 5.0 / 6.0, 5.0 / 6.0, 1.0 / 6.0)
    for c in range(4):
        points = [4 * i + j for i in range(4) for j in range(4) if 2 * (i // 2) + j // 2 == c]
        for r in range(3):
            value = weighted(
                [(quad[p // 4] * quad[p % 4], state[:, slab(p, 2 + r)]) for p in points]
            )
            if r > 0:
                value = jnp.maximum(value, 0.0) + jnp.log1p(jnp.exp(-jnp.abs(value)))
            cols[r, pl.ds(NE * c, NE), :] = value
    for r in range(2):
        turned = cols[r + 1].T
        high = turned.astype(BF16).astype(F32)
        wt[2 * r] = high
        wt[2 * r + 1] = turned - high

    row_in_16 = lax.broadcasted_iota(jnp.int32, (128, NL), 0) % 16
    scale = -math.log2(math.e)

    def depth_group(group, _):
        rows = pl.ds(pl.multiple_of(16 * group, 16), 16)
        kw_f = kw[rows, :] * scale
        kt_f = kt[rows, :] * scale
        kw_h = kw_f.astype(BF16).astype(F32)
        kt_h = kt_f.astype(BF16).astype(F32)
        zero = jnp.zeros((32, NL), F32)
        k_stack = jnp.concatenate(
            [kw_h, kw_h, kw_f - kw_h, kt_h, kt_h, kt_f - kt_h, zero], axis=0
        )
        k_turned = k_stack.T.astype(BF16)
        w_h, w_l, t_h, t_l = (wt[i, rows, :] for i in range(4))
        w_stack = jnp.concatenate([w_h, w_l, w_h, t_h, t_l, t_h, zero], axis=0)
        for i in range(16):
            one = jnp.where(row_in_16 == i, w_stack, 0.0).astype(BF16)
            power = jnp.dot(k_turned, one, preferred_element_type=F32)
            passed = jnp.exp2(power)
            level = 16 * group + i
            tran[level] = passed
            st_part[pl.ds(pl.multiple_of(8 * level, 8), 8), :] = fold(passed)
        return 0

    half = NL // 32
    pl.semaphore_wait(z_mid, 2)
    tell(z_far, z_peer(2))
    tell(z_far, z_peer(-2))
    lax.fori_loop(0, half, depth_group, 0)
    pl.semaphore_wait(z_far, 2)
    pl.semaphore_wait(x_near, 2)
    z_copies = []
    for j in range(1, nz):
        copy = pltpu.make_async_remote_copy(
            src_ref=surface,
            dst_ref=zbuf.at[my_z],
            send_sem=z_send.at[j - 1],
            recv_sem=z_recv.at[j - 1],
            device_id=z_peer(j),
            device_id_type=MESH,
        )
        copy.start()
        z_copies.append(copy)
    for v in SEND_ORDER[2:]:
        send_rim(v)
    lax.fori_loop(half, 2 * half, depth_group, 0)

    def march(level, carry):
        down, up = carry
        back = NL - 1 - level
        down = down * tran[level]
        sp_part[pl.ds(pl.multiple_of(8 * level, 8), 8), :] = fold(down)
        sq_part[pl.ds(pl.multiple_of(8 * back, 8), 8), :] = fold(up)
        up = up * tran[back]
        return down, up

    ones = jnp.ones((NL, NL), F32)
    lax.fori_loop(0, NL, march, (ones, ones))

    keep.wait()
    for copy in z_copies:
        copy.wait()
    x_copies = []
    keep_x = pltpu.make_async_copy(zbuf, xbuf.at[my_x], copy_sem.at[1])
    keep_x.start()
    for j in range(1, nx):
        copy = pltpu.make_async_remote_copy(
            src_ref=zbuf,
            dst_ref=xbuf.at[my_x],
            send_sem=x_send.at[j - 1],
            recv_sem=x_recv.at[j - 1],
            device_id=x_peer(j),
            device_id_type=MESH,
        )
        copy.start()
        x_copies.append(copy)

    def total(part):
        return sum(part[pl.ds(s, NL, stride=8), :] for s in range(8))

    sum_t, sum_p, sum_q = total(st_part), total(sp_part), total(sq_part)
    shift[0, pl.ds(0, 8), :] = jnp.full((8, NL), float(NL), F32)
    shift[0, pl.ds(8, NL), :] = sum_p
    shift[1, pl.ds(0, 8), :] = jnp.broadcast_to(sum_p[NL - 1 : NL], (8, NL))
    shift[1, pl.ds(8, NL), :] = sum_q
    inv = 1.0 / NL
    downward = ((shift[0, pl.ds(7, NL), :] - sum_p) * (64.0 * inv)).T
    upward = ((sum_q - shift[1, pl.ds(7, NL), :]) * (2.0 * inv)).T
    emitted = (8.0 - sum_t * (8.0 * inv)).T

    base = me * NE - NE
    elems = n_dev * NE
    local = nbr[...] - base
    local = jnp.where(local < 0, local + elems, local)
    local = jnp.where(local >= elems, local - elems, local)
    target = nedge[...] * 192 + local
    lane = lax.broadcasted_iota(jnp.int32, (NE, 768), 1)
    sub = lax.broadcasted_iota(jnp.int32, (NE, NE), 0)
    lan = lax.broadcasted_iota(jnp.int32, (NE, NE), 1)

    def column(row):
        return jnp.sum(jnp.where(sub == lan, row, 0.0), axis=1, keepdims=True)

    for k in range(4):
        row = jnp.broadcast_to(target[k : k + 1, :].astype(F32), (NE, NE))
        want = column(row).astype(jnp.int32)
        hit = (lane == want) | (lane == want + 96)
        onehot[pl.ds(NE * k, NE), :] = hit.astype(F32).astype(BF16)

    own_row = jnp.broadcast_to(owner[...].astype(F32), (NE, NE))
    own_col = column(own_row)
    earlier = (own_col == own_row) & (lan < sub)
    rank = jnp.sum(jnp.where(earlier, 1.0, 0.0), axis=1, keepdims=True).astype(jnp.int32)

    keep_x.wait()
    for copy in x_copies:
        copy.wait()
    width = surface.shape[1]
    owner_wide = jnp.broadcast_to(own_col.astype(jnp.int32), (NE, width))
    picked = jnp.zeros((NE, width), F32)
    for x in range(nx):
        for z in range(nz):
            row = jnp.broadcast_to(xbuf[x, z], (NE, width))
            picked = jnp.where(owner_wide == x * nz + z, row, picked)
    s_lane = lax.broadcasted_iota(jnp.int32, (NE, width), 1)
    first = (cur * (width // (4 * n_cur)) + rank) * 4
    heat = []
    for c in range(4):
        surf = jnp.sum(jnp.where(s_lane == first + c, picked, 0.0), axis=1, keepdims=True)
        part = slice(NE * c, NE * c + NE)
        heat.append(
            0.2
            * (
                downward[part]
                + surf * upward[part]
                - jnp.tanh(cols[0, pl.ds(NE * c, NE), :]) * emitted[part]
            )
        )

    count = [1 + sum(p in edge for edge in EDGES) for p in range(16)]
    for v in SEND_ORDER:
        rim_copies[0, v].wait()
        rim_copies[1, v].wait()
        for f in range(4):
            for m in range(4):
                b = RIM.index(EDGES[f][3 - m])
                lanes = pl.ds(NL * m, NL)
                for s, ref in enumerate((left, own, right)):
                    high, low = split(ref[v, b])
                    rhs[pl.ds(192 * f + 32 * s, 32), lanes] = high
                    rhs[pl.ds(192 * f + 96 + 32 * s, 32), lanes] = low
        got = jnp.dot(onehot[...], rhs[...], preferred_element_type=F32)
        for p in range(16):
            if p in RIM:
                tend = own[v, RIM.index(p)]
            else:
                tend = inner[v, INNER.index(p)]
            for k in range(4):
                if p in EDGES[k]:
                    m = EDGES[k].index(p)
                    tend = tend + got[NE * k : NE * k + NE, NL * m : NL * m + NL]
            value = state[:, slab(p, v)] + tend * (0.2 / count[p])
            if v == 2:
                value = value + heat[2 * (p // 8) + (p % 4) // 2]
            out[:, slab(p, v)] = value


def per_device(nx, nz, state, neighbour, neighbour_edge, owner, surface, k_water, k_tracer):
    width = surface.shape[1]
    vmem = pl.BlockSpec(memory_space=pltpu.VMEM)
    anywhere = pl.BlockSpec(memory_space=pl.ANY)
    args = (state, neighbour.T, neighbour_edge.T, owner.T, surface, k_water, k_tracer)
    sem = pltpu.SemaphoreType.DMA
    return pl.pallas_call(
        functools.partial(kernel, nx, nz),
        out_shape=pltpu.VMEM(state.shape, F32),
        in_specs=[anywhere] * 7,
        out_specs=vmem,
        scratch_shapes=[
            *[pltpu.VMEM(arg.shape, arg.dtype) for arg in args],
            pltpu.VMEM((NV, 12, NE, NL), F32),
            pltpu.VMEM((NV, 12, NE, NL), F32),
            pltpu.VMEM((NV, 12, NE, NL), F32),
            pltpu.VMEM((NV, 4, NE, NL), F32),
            pltpu.VMEM((3, NL, NL), F32),
            pltpu.VMEM((4, NL, NL), F32),
            pltpu.VMEM((NL, NL, NL), F32),
            pltpu.VMEM((8 * NL, NL), F32),
            pltpu.VMEM((8 * NL, NL), F32),
            pltpu.VMEM((8 * NL, NL), F32),
            pltpu.VMEM((2, NL + 8, NL), F32),
            pltpu.VMEM((NL, 768), BF16),
            pltpu.VMEM((768, 512), BF16),
            pltpu.VMEM((nz, 1, width), F32),
            pltpu.VMEM((nx, nz, 1, width), F32),
            sem((2, NV)),
            sem((2, NV)),
            sem((max(nz - 1, 1),)),
            sem((max(nz - 1, 1),)),
            sem((max(nx - 1, 1),)),
            sem((max(nx - 1, 1),)),
            sem((2,)),
            sem((7,)),
            *[pltpu.SemaphoreType.REGULAR] * 4,
        ],
        compiler_params=pltpu.CompilerParams(collective_id=0, has_side_effects=True),
        name="dynamics_physics",
    )(*args)


def solution(mesh):
    n_cur = mesh.shape["cur"]
    nx = 4 if n_cur % 4 == 0 and n_cur > 4 else 2
    nz = n_cur // nx
    both = P(("blk", "cur"), None)
    return jax.shard_map(
        functools.partial(per_device, nx, nz),
        mesh=mesh,
        in_specs=(both, both, both, both, both, P(), P()),
        out_specs=both,
        check_vma=False,
    )
```

```python
import functools
import math

import jax
import jax.numpy as jnp
import numpy as np
from jax import lax
from jax.experimental import pallas as pl
from jax.experimental.pallas import tpu as pltpu
from jax.sharding import PartitionSpec as P

MESH = pl.DeviceIdType.MESH
F32 = jnp.float32
BF16 = jnp.bfloat16
EDGES = ((0, 4, 8, 12), (12, 13, 14, 15), (15, 11, 7, 3), (3, 2, 1, 0))
RIM = (0, 1, 2, 3, 4, 7, 8, 11, 12, 13, 14, 15)
INNER = (5, 6, 9, 10)
SEND_ORDER = (0, 1, 3, 4, 2)
NE = 32
NV = 5
NL = 128


def gll_matrix():
    nodes = np.array([-1.0, -1.0 / np.sqrt(5.0), 1.0 / np.sqrt(5.0), 1.0])
    weights = np.array(
        [1.0 / np.prod([nodes[c] - nodes[o] for o in range(4) if o != c]) for c in range(4)]
    )
    matrix = np.zeros((4, 4))
    for r in range(4):
        for c in range(4):
            if r != c:
                matrix[r, c] = weights[c] / weights[r] / (nodes[r] - nodes[c])
        matrix[r, r] = -np.sum(matrix[r])
    return matrix


def weighted(terms):
    total = None
    for weight, value in terms:
        if abs(weight) < 1e-12:
            continue
        part = value * float(weight)
        total = part if total is None else total + part
    return total


def slab(p, v):
    return pl.ds((p * NV + v) * NL, NL)


def split(x):
    high = x.astype(BF16)
    low = (x - high.astype(F32)).astype(BF16)
    return high, low


def fold(x):
    rows = x.shape[0] // 8
    parts = [x[8 * i : 8 * i + 8] for i in range(rows)]
    while len(parts) > 1:
        parts = [parts[i] + parts[i + 1] for i in range(0, len(parts), 2)]
    return parts[0]


def kernel(
    nx,
    nz,
    state_in,
    nbr_in,
    nedge_in,
    owner_in,
    surface_in,
    kw_in,
    kt_in,
    out,
    state,
    nbr,
    nedge,
    owner,
    surface,
    kw,
    kt,
    own,
    left,
    right,
    inner,
    cols,
    wt,
    tran,
    st_part,
    sp_part,
    sq_part,
    shift,
    onehot,
    rhs,
    zbuf,
    xbuf,
    rim_send,
    rim_recv,
    z_send,
    z_recv,
    x_send,
    x_recv,
    copy_sem,
    load_sem,
    z_near,
    z_mid,
    z_far,
    x_near,
):
    blk = lax.axis_index("blk")
    cur = lax.axis_index("cur")
    n_blk = lax.axis_size("blk")
    n_cur = nx * nz
    n_dev = n_blk * n_cur
    me = blk * n_cur + cur
    my_x = cur // nz
    my_z = cur % nz

    def place(index):
        return (index // n_cur, index % n_cur)

    after = place(lax.rem(me + 1, n_dev))
    before = place(lax.rem(me + n_dev - 1, n_dev))

    def z_peer(j):
        return (blk, my_x * nz + lax.rem(my_z + j + nz, nz))

    def x_peer(j):
        return (blk, lax.rem(my_x + j + nx, nx) * nz + my_z)

    def tell(sem, peer):
        pl.semaphore_signal(sem, inc=1, device_id=peer, device_id_type=MESH)

    barrier = pltpu.get_barrier_semaphore()
    peers = [after, before, z_peer(1), z_peer(-1), x_peer(1), x_peer(-1)]
    for peer in peers:
        tell(barrier, peer)
    loads = []
    pairs = (
        (state_in, state),
        (surface_in, surface),
        (kw_in, kw),
        (kt_in, kt),
        (nbr_in, nbr),
        (nedge_in, nedge),
        (owner_in, owner),
    )
    for i, (src, dst) in enumerate(pairs):
        load = pltpu.make_async_copy(src, dst, load_sem.at[i])
        load.start()
        loads.append(load)
    loads[0].wait()

    d_matrix = -0.5 * gll_matrix()

    def tend_rows(v, g, _):
        rows = pl.ds(pl.multiple_of(8 * g, 8), 8)
        q = [state[rows, slab(p, v)] for p in range(16)]
        for i in range(4):
            for j in range(4):
                p = 4 * i + j
                qx = weighted([(d_matrix[i, a], q[4 * a + j]) for a in range(4)])
                qy = weighted([(d_matrix[j, b], q[4 * i + b]) for b in range(4)])
                tend = state[rows, slab(p, 0)] * qx + state[rows, slab(p, 1)] * qy
                if p in RIM:
                    own[v, RIM.index(p), rows, :] = tend
                else:
                    inner[v, INNER.index(p), rows, :] = tend
        return 0

    def tend_of(v):
        lax.fori_loop(0, NE // 8, functools.partial(tend_rows, v), 0)

    rim_copies = {}

    def send_rim(v):
        for side, (dst, peer) in enumerate(((left, after), (right, before))):
            copy = pltpu.make_async_remote_copy(
                src_ref=own.at[v],
                dst_ref=dst.at[v],
                send_sem=rim_send.at[side, v],
                recv_sem=rim_recv.at[side, v],
                device_id=peer,
                device_id_type=MESH,
            )
            copy.start()
            rim_copies[side, v] = copy

    tend_of(SEND_ORDER[0])
    pl.semaphore_wait(barrier, len(peers))
    tell(z_near, z_peer(1))
    tell(z_near, z_peer(-1))
    tell(x_near, x_peer(1))
    tell(x_near, x_peer(-1))
    send_rim(SEND_ORDER[0])
    for load in loads[1:]:
        load.wait()
    keep = pltpu.make_async_copy(surface, zbuf.at[my_z], copy_sem.at[0])
    keep.start()
    pl.semaphore_wait(z_near, 2)
    tell(z_mid, z_peer(2))
    tell(z_mid, z_peer(-2))
    for v in SEND_ORDER[1:]:
        tend_of(v)

    quad = (1.0 / 6.0, 5.0 / 6.0, 5.0 / 6.0, 1.0 / 6.0)
    for c in range(4):
        points = [4 * i + j for i in range(4) for j in range(4) if 2 * (i // 2) + j // 2 == c]
        for r in range(3):
            value = weighted(
                [(quad[p // 4] * quad[p % 4], state[:, slab(p, 2 + r)]) for p in points]
            )
            if r > 0:
                value = jnp.maximum(value, 0.0) + jnp.log1p(jnp.exp(-jnp.abs(value)))
            cols[r, pl.ds(NE * c, NE), :] = value
    for r in range(2):
        turned = cols[r + 1].T
        high = turned.astype(BF16).astype(F32)
        wt[2 * r] = high
        wt[2 * r + 1] = turned - high

    row_in_16 = lax.broadcasted_iota(jnp.int32, (128, NL), 0) % 16
    scale = -math.log2(math.e)

    def depth_group(group, _):
        rows = pl.ds(pl.multiple_of(16 * group, 16), 16)
        kw_f = kw[rows, :] * scale
        kt_f = kt[rows, :] * scale
        kw_h = kw_f.astype(BF16).astype(F32)
        kt_h = kt_f.astype(BF16).astype(F32)
        zero = jnp.zeros((32, NL), F32)
        k_stack = jnp.concatenate(
            [kw_h, kw_h, kw_f - kw_h, kt_h, kt_h, kt_f - kt_h, zero], axis=0
        )
        k_turned = k_stack.T.astype(BF16)
        w_h, w_l, t_h, t_l = (wt[i, rows, :] for i in range(4))
        w_stack = jnp.concatenate([w_h, w_l, w_h, t_h, t_l, t_h, zero], axis=0)
        for i in range(16):
            one = jnp.where(row_in_16 == i, w_stack, 0.0).astype(BF16)
            power = jnp.dot(k_turned, one, preferred_element_type=F32)
            passed = jnp.exp2(power)
            level = 16 * group + i
            tran[level] = passed
            st_part[pl.ds(pl.multiple_of(8 * level, 8), 8), :] = fold(passed)
        return 0

    half = NL // 32
    pl.semaphore_wait(z_mid, 2)
    tell(z_far, z_peer(2))
    tell(z_far, z_peer(-2))
    lax.fori_loop(0, half, depth_group, 0)
    pl.semaphore_wait(z_far, 2)
    pl.semaphore_wait(x_near, 2)
    z_copies = []
    for j in range(1, nz):
        copy = pltpu.make_async_remote_copy(
            src_ref=surface,
            dst_ref=zbuf.at[my_z],
            send_sem=z_send.at[j - 1],
            recv_sem=z_recv.at[j - 1],
            device_id=z_peer(j),
            device_id_type=MESH,
        )
        copy.start()
        z_copies.append(copy)
    for v in SEND_ORDER[1:]:
        send_rim(v)
    lax.fori_loop(half, 2 * half, depth_group, 0)

    def march(level, carry):
        down, up = carry
        back = NL - 1 - level
        down = down * tran[level]
        sp_part[pl.ds(pl.multiple_of(8 * level, 8), 8), :] = fold(down)
        sq_part[pl.ds(pl.multiple_of(8 * back, 8), 8), :] = fold(up)
        up = up * tran[back]
        return down, up

    ones = jnp.ones((NL, NL), F32)
    lax.fori_loop(0, NL, march, (ones, ones))

    keep.wait()
    for copy in z_copies:
        copy.wait()
    x_copies = []
    keep_x = pltpu.make_async_copy(zbuf, xbuf.at[my_x], copy_sem.at[1])
    keep_x.start()
    for j in range(1, nx):
        copy = pltpu.make_async_remote_copy(
            src_ref=zbuf,
            dst_ref=xbuf.at[my_x],
            send_sem=x_send.at[j - 1],
            recv_sem=x_recv.at[j - 1],
            device_id=x_peer(j),
            device_id_type=MESH,
        )
        copy.start()
        x_copies.append(copy)

    def total(part):
        return sum(part[pl.ds(s, NL, stride=8), :] for s in range(8))

    sum_t, sum_p, sum_q = total(st_part), total(sp_part), total(sq_part)
    shift[0, pl.ds(0, 8), :] = jnp.full((8, NL), float(NL), F32)
    shift[0, pl.ds(8, NL), :] = sum_p
    shift[1, pl.ds(0, 8), :] = jnp.broadcast_to(sum_p[NL - 1 : NL], (8, NL))
    shift[1, pl.ds(8, NL), :] = sum_q
    inv = 1.0 / NL
    downward = ((shift[0, pl.ds(7, NL), :] - sum_p) * (64.0 * inv)).T
    upward = ((sum_q - shift[1, pl.ds(7, NL), :]) * (2.0 * inv)).T
    emitted = (8.0 - sum_t * (8.0 * inv)).T

    base = me * NE - NE
    elems = n_dev * NE
    local = nbr[...] - base
    local = jnp.where(local < 0, local + elems, local)
    local = jnp.where(local >= elems, local - elems, local)
    target = nedge[...] * 192 + local
    lane = lax.broadcasted_iota(jnp.int32, (NE, 768), 1)
    sub = lax.broadcasted_iota(jnp.int32, (NE, NE), 0)
    lan = lax.broadcasted_iota(jnp.int32, (NE, NE), 1)

    def column(row):
        return jnp.sum(jnp.where(sub == lan, row, 0.0), axis=1, keepdims=True)

    for k in range(4):
        row = jnp.broadcast_to(target[k : k + 1, :].astype(F32), (NE, NE))
        want = column(row).astype(jnp.int32)
        hit = (lane == want) | (lane == want + 96)
        onehot[pl.ds(NE * k, NE), :] = hit.astype(F32).astype(BF16)

    own_row = jnp.broadcast_to(owner[...].astype(F32), (NE, NE))
    own_col = column(own_row)
    earlier = (own_col == own_row) & (lan < sub)
    rank = jnp.sum(jnp.where(earlier, 1.0, 0.0), axis=1, keepdims=True).astype(jnp.int32)

    def heating():
        keep_x.wait()
        for copy in x_copies:
            copy.wait()
        width = surface.shape[1]
        owner_wide = jnp.broadcast_to(own_col.astype(jnp.int32), (NE, width))
        picked = jnp.zeros((NE, width), F32)
        for x in range(nx):
            for z in range(nz):
                row = jnp.broadcast_to(xbuf[x, z], (NE, width))
                picked = jnp.where(owner_wide == x * nz + z, row, picked)
        s_lane = lax.broadcasted_iota(jnp.int32, (NE, width), 1)
        first = (cur * (width // (4 * n_cur)) + rank) * 4
        heat = []
        for c in range(4):
            surf = jnp.sum(jnp.where(s_lane == first + c, picked, 0.0), axis=1, keepdims=True)
            part = slice(NE * c, NE * c + NE)
            heat.append(
                0.2
                * (
                    downward[part]
                    + surf * upward[part]
                    - jnp.tanh(cols[0, pl.ds(NE * c, NE), :]) * emitted[part]
                )
            )
        return heat

    count = [1 + sum(p in edge for edge in EDGES) for p in range(16)]
    for v in SEND_ORDER:
        rim_copies[0, v].wait()
        rim_copies[1, v].wait()
        for f in range(4):
            for m in range(4):
                b = RIM.index(EDGES[f][3 - m])
                lanes = pl.ds(NL * m, NL)
                for s, ref in enumerate((left, own, right)):
                    high, low = split(ref[v, b])
                    rhs[pl.ds(192 * f + 32 * s, 32), lanes] = high
                    rhs[pl.ds(192 * f + 96 + 32 * s, 32), lanes] = low
        if v == 2:
            heat = heating()
        got = jnp.dot(onehot[...], rhs[...], preferred_element_type=F32)
        for p in range(16):
            if p in RIM:
                tend = own[v, RIM.index(p)]
            else:
                tend = inner[v, INNER.index(p)]
            for k in range(4):
                if p in EDGES[k]:
                    m = EDGES[k].index(p)
                    tend = tend + got[NE * k : NE * k + NE, NL * m : NL * m + NL]
            value = state[:, slab(p, v)] + tend * (0.2 / count[p])
            if v == 2:
                value = value + heat[2 * (p // 8) + (p % 4) // 2]
            out[:, slab(p, v)] = value


def per_device(nx, nz, state, neighbour, neighbour_edge, owner, surface, k_water, k_tracer):
    width = surface.shape[1]
    vmem = pl.BlockSpec(memory_space=pltpu.VMEM)
    anywhere = pl.BlockSpec(memory_space=pl.ANY)
    args = (state, neighbour.T, neighbour_edge.T, owner.T, surface, k_water, k_tracer)
    sem = pltpu.SemaphoreType.DMA
    return pl.pallas_call(
        functools.partial(kernel, nx, nz),
        out_shape=pltpu.VMEM(state.shape, F32),
        in_specs=[anywhere] * 7,
        out_specs=vmem,
        scratch_shapes=[
            *[pltpu.VMEM(arg.shape, arg.dtype) for arg in args],
            pltpu.VMEM((NV, 12, NE, NL), F32),
            pltpu.VMEM((NV, 12, NE, NL), F32),
            pltpu.VMEM((NV, 12, NE, NL), F32),
            pltpu.VMEM((NV, 4, NE, NL), F32),
            pltpu.VMEM((3, NL, NL), F32),
            pltpu.VMEM((4, NL, NL), F32),
            pltpu.VMEM((NL, NL, NL), F32),
            pltpu.VMEM((8 * NL, NL), F32),
            pltpu.VMEM((8 * NL, NL), F32),
            pltpu.VMEM((8 * NL, NL), F32),
            pltpu.VMEM((2, NL + 8, NL), F32),
            pltpu.VMEM((NL, 768), BF16),
            pltpu.VMEM((768, 512), BF16),
            pltpu.VMEM((nz, 1, width), F32),
            pltpu.VMEM((nx, nz, 1, width), F32),
            sem((2, NV)),
            sem((2, NV)),
            sem((max(nz - 1, 1),)),
            sem((max(nz - 1, 1),)),
            sem((max(nx - 1, 1),)),
            sem((max(nx - 1, 1),)),
            sem((2,)),
            sem((7,)),
            *[pltpu.SemaphoreType.REGULAR] * 4,
        ],
        compiler_params=pltpu.CompilerParams(collective_id=0, has_side_effects=True),
        name="dynamics_physics",
    )(*args)


def solution(mesh):
    n_cur = mesh.shape["cur"]
    nx = 4 if n_cur % 4 == 0 and n_cur > 4 else 2
    nz = n_cur // nx
    both = P(("blk", "cur"), None)
    return jax.shard_map(
        functools.partial(per_device, nx, nz),
        mesh=mesh,
        in_specs=(both, both, both, both, both, P(), P()),
        out_specs=both,
        check_vma=False,
    )
```

```python
import functools
import math

import jax
import jax.numpy as jnp
import numpy as np
from jax import lax
from jax.experimental import pallas as pl
from jax.experimental.pallas import tpu as pltpu
from jax.sharding import PartitionSpec as P

MESH = pl.DeviceIdType.MESH
F32 = jnp.float32
BF16 = jnp.bfloat16
EDGES = ((0, 4, 8, 12), (12, 13, 14, 15), (15, 11, 7, 3), (3, 2, 1, 0))
RIM = (0, 1, 2, 3, 4, 7, 8, 11, 12, 13, 14, 15)
INNER = (5, 6, 9, 10)
SEND_ORDER = (0, 1, 3, 4, 2)
EARLY = 3
NE = 32
NV = 5
NL = 128


def gll_matrix():
    nodes = np.array([-1.0, -1.0 / np.sqrt(5.0), 1.0 / np.sqrt(5.0), 1.0])
    weights = np.array(
        [1.0 / np.prod([nodes[c] - nodes[o] for o in range(4) if o != c]) for c in range(4)]
    )
    matrix = np.zeros((4, 4))
    for r in range(4):
        for c in range(4):
            if r != c:
                matrix[r, c] = weights[c] / weights[r] / (nodes[r] - nodes[c])
        matrix[r, r] = -np.sum(matrix[r])
    return matrix


def weighted(terms):
    total = None
    for weight, value in terms:
        if abs(weight) < 1e-12:
            continue
        part = value * float(weight)
        total = part if total is None else total + part
    return total


def slab(p, v):
    return pl.ds((p * NV + v) * NL, NL)


def split(x):
    high = x.astype(BF16)
    low = (x - high.astype(F32)).astype(BF16)
    return high, low


def fold(x):
    rows = x.shape[0] // 8
    parts = [x[8 * i : 8 * i + 8] for i in range(rows)]
    while len(parts) > 1:
        parts = [parts[i] + parts[i + 1] for i in range(0, len(parts), 2)]
    return parts[0]


def kernel(
    nx,
    nz,
    state_in,
    nbr_in,
    nedge_in,
    owner_in,
    surface_in,
    kw_in,
    kt_in,
    out,
    state,
    nbr,
    nedge,
    owner,
    surface,
    kw,
    kt,
    own,
    left,
    right,
    inner,
    cols,
    wt,
    tran,
    st_part,
    sp_part,
    sq_part,
    shift,
    onehot,
    rhs,
    zbuf,
    xbuf,
    rim_send,
    rim_recv,
    z_send,
    z_recv,
    x_send,
    x_recv,
    copy_sem,
    row_sem,
    load_sem,
    z_near,
    z_mid,
    z_far,
    x_near,
):
    blk = lax.axis_index("blk")
    cur = lax.axis_index("cur")
    n_blk = lax.axis_size("blk")
    n_cur = nx * nz
    n_dev = n_blk * n_cur
    me = blk * n_cur + cur
    my_x = cur // nz
    my_z = cur % nz

    def place(index):
        return (index // n_cur, index % n_cur)

    after = place(lax.rem(me + 1, n_dev))
    before = place(lax.rem(me + n_dev - 1, n_dev))

    def z_peer(j):
        return (blk, my_x * nz + lax.rem(my_z + j + nz, nz))

    def x_peer(j):
        return (blk, lax.rem(my_x + j + nx, nx) * nz + my_z)

    def tell(sem, peer):
        pl.semaphore_signal(sem, inc=1, device_id=peer, device_id_type=MESH)

    barrier = pltpu.get_barrier_semaphore()
    peers = [after, before, z_peer(1), z_peer(-1), x_peer(1), x_peer(-1)]
    for peer in peers:
        tell(barrier, peer)
    loads = []
    rows_in = []
    for g in range(NE // 8):
        rows = pl.ds(8 * g, 8)
        load = pltpu.make_async_copy(state_in.at[rows, :], state.at[rows, :], row_sem.at[g])
        load.start()
        rows_in.append(load)
    pairs = (
        (surface_in, surface),
        (kw_in, kw),
        (kt_in, kt),
        (nbr_in, nbr),
        (nedge_in, nedge),
        (owner_in, owner),
    )
    for i, (src, dst) in enumerate(pairs):
        load = pltpu.make_async_copy(src, dst, load_sem.at[i])
        load.start()
        loads.append(load)

    d_matrix = -0.5 * gll_matrix()

    def tend_rows(v, g, _):
        rows = pl.ds(pl.multiple_of(8 * g, 8), 8)
        q = [state[rows, slab(p, v)] for p in range(16)]
        for i in range(4):
            for j in range(4):
                p = 4 * i + j
                qx = weighted([(d_matrix[i, a], q[4 * a + j]) for a in range(4)])
                qy = weighted([(d_matrix[j, b], q[4 * i + b]) for b in range(4)])
                tend = state[rows, slab(p, 0)] * qx + state[rows, slab(p, 1)] * qy
                if p in RIM:
                    own[v, RIM.index(p), rows, :] = tend
                else:
                    inner[v, INNER.index(p), rows, :] = tend
        return 0

    def tend_of(v):
        lax.fori_loop(0, NE // 8, functools.partial(tend_rows, v), 0)

    rim_copies = {}

    def send_rim(v):
        for side, (dst, peer) in enumerate(((left, after), (right, before))):
            copy = pltpu.make_async_remote_copy(
                src_ref=own.at[v],
                dst_ref=dst.at[v],
                send_sem=rim_send.at[side, v],
                recv_sem=rim_recv.at[side, v],
                device_id=peer,
                device_id_type=MESH,
            )
            copy.start()
            rim_copies[side, v] = copy

    for g in range(NE // 8):
        rows_in[g].wait()
        tend_rows(SEND_ORDER[0], g, 0)
    pl.semaphore_wait(barrier, len(peers))
    tell(z_near, z_peer(1))
    tell(z_near, z_peer(-1))
    tell(x_near, x_peer(1))
    tell(x_near, x_peer(-1))
    send_rim(SEND_ORDER[0])
    for v in SEND_ORDER[1:EARLY]:
        tend_of(v)
        send_rim(v)
    for load in loads:
        load.wait()
    keep = pltpu.make_async_copy(surface, zbuf.at[my_z], copy_sem.at[0])
    keep.start()
    pl.semaphore_wait(z_near, 2)
    tell(z_mid, z_peer(2))
    tell(z_mid, z_peer(-2))
    for v in SEND_ORDER[EARLY:]:
        tend_of(v)

    quad = (1.0 / 6.0, 5.0 / 6.0, 5.0 / 6.0, 1.0 / 6.0)
    for c in range(4):
        points = [4 * i + j for i in range(4) for j in range(4) if 2 * (i // 2) + j // 2 == c]
        for r in range(3):
            value = weighted(
                [(quad[p // 4] * quad[p % 4], state[:, slab(p, 2 + r)]) for p in points]
            )
            if r > 0:
                value = jnp.maximum(value, 0.0) + jnp.log1p(jnp.exp(-jnp.abs(value)))
            cols[r, pl.ds(NE * c, NE), :] = value
    for r in range(2):
        turned = cols[r + 1].T
        high = turned.astype(BF16).astype(F32)
        wt[2 * r] = high
        wt[2 * r + 1] = turned - high

    row_in_16 = lax.broadcasted_iota(jnp.int32, (128, NL), 0) % 16
    scale = -math.log2(math.e)

    def depth_group(group, _):
        rows = pl.ds(pl.multiple_of(16 * group, 16), 16)
        kw_f = kw[rows, :] * scale
        kt_f = kt[rows, :] * scale
        kw_h = kw_f.astype(BF16).astype(F32)
        kt_h = kt_f.astype(BF16).astype(F32)
        zero = jnp.zeros((32, NL), F32)
        k_stack = jnp.concatenate(
            [kw_h, kw_h, kw_f - kw_h, kt_h, kt_h, kt_f - kt_h, zero], axis=0
        )
        k_turned = k_stack.T.astype(BF16)
        w_h, w_l, t_h, t_l = (wt[i, rows, :] for i in range(4))
        w_stack = jnp.concatenate([w_h, w_l, w_h, t_h, t_l, t_h, zero], axis=0)
        for i in range(16):
            one = jnp.where(row_in_16 == i, w_stack, 0.0).astype(BF16)
            power = jnp.dot(k_turned, one, preferred_element_type=F32)
            passed = jnp.exp2(power)
            level = 16 * group + i
            tran[level] = passed
            st_part[pl.ds(pl.multiple_of(8 * level, 8), 8), :] = fold(passed)
        return 0

    half = NL // 32
    pl.semaphore_wait(z_mid, 2)
    tell(z_far, z_peer(2))
    tell(z_far, z_peer(-2))
    lax.fori_loop(0, half, depth_group, 0)
    pl.semaphore_wait(z_far, 2)
    pl.semaphore_wait(x_near, 2)
    z_copies = []
    for j in range(1, nz):
        copy = pltpu.make_async_remote_copy(
            src_ref=surface,
            dst_ref=zbuf.at[my_z],
            send_sem=z_send.at[j - 1],
            recv_sem=z_recv.at[j - 1],
            device_id=z_peer(j),
            device_id_type=MESH,
        )
        copy.start()
        z_copies.append(copy)
    for v in SEND_ORDER[EARLY:]:
        send_rim(v)
    lax.fori_loop(half, 2 * half, depth_group, 0)

    def march(level, carry):
        down, up = carry
        back = NL - 1 - level
        down = down * tran[level]
        sp_part[pl.ds(pl.multiple_of(8 * level, 8), 8), :] = fold(down)
        sq_part[pl.ds(pl.multiple_of(8 * back, 8), 8), :] = fold(up)
        up = up * tran[back]
        return down, up

    ones = jnp.ones((NL, NL), F32)
    lax.fori_loop(0, NL, march, (ones, ones))

    keep.wait()
    for copy in z_copies:
        copy.wait()
    x_copies = []
    keep_x = pltpu.make_async_copy(zbuf, xbuf.at[my_x], copy_sem.at[1])
    keep_x.start()
    for j in range(1, nx):
        copy = pltpu.make_async_remote_copy(
            src_ref=zbuf,
            dst_ref=xbuf.at[my_x],
            send_sem=x_send.at[j - 1],
            recv_sem=x_recv.at[j - 1],
            device_id=x_peer(j),
            device_id_type=MESH,
        )
        copy.start()
        x_copies.append(copy)

    def total(part):
        return sum(part[pl.ds(s, NL, stride=8), :] for s in range(8))

    sum_t, sum_p, sum_q = total(st_part), total(sp_part), total(sq_part)
    shift[0, pl.ds(0, 8), :] = jnp.full((8, NL), float(NL), F32)
    shift[0, pl.ds(8, NL), :] = sum_p
    shift[1, pl.ds(0, 8), :] = jnp.broadcast_to(sum_p[NL - 1 : NL], (8, NL))
    shift[1, pl.ds(8, NL), :] = sum_q
    inv = 1.0 / NL
    downward = ((shift[0, pl.ds(7, NL), :] - sum_p) * (64.0 * inv)).T
    upward = ((sum_q - shift[1, pl.ds(7, NL), :]) * (2.0 * inv)).T
    emitted = (8.0 - sum_t * (8.0 * inv)).T

    base = me * NE - NE
    elems = n_dev * NE
    local = nbr[...] - base
    local = jnp.where(local < 0, local + elems, local)
    local = jnp.where(local >= elems, local - elems, local)
    target = nedge[...] * 192 + local
    lane = lax.broadcasted_iota(jnp.int32, (NE, 768), 1)
    sub = lax.broadcasted_iota(jnp.int32, (NE, NE), 0)
    lan = lax.broadcasted_iota(jnp.int32, (NE, NE), 1)

    def column(row):
        return jnp.sum(jnp.where(sub == lan, row, 0.0), axis=1, keepdims=True)

    for k in range(4):
        row = jnp.broadcast_to(target[k : k + 1, :].astype(F32), (NE, NE))
        want = column(row).astype(jnp.int32)
        hit = (lane == want) | (lane == want + 96)
        onehot[pl.ds(NE * k, NE), :] = hit.astype(F32).astype(BF16)

    own_row = jnp.broadcast_to(owner[...].astype(F32), (NE, NE))
    own_col = column(own_row)
    earlier = (own_col == own_row) & (lan < sub)
    rank = jnp.sum(jnp.where(earlier, 1.0, 0.0), axis=1, keepdims=True).astype(jnp.int32)

    def heating():
        keep_x.wait()
        for copy in x_copies:
            copy.wait()
        width = surface.shape[1]
        owner_wide = jnp.broadcast_to(own_col.astype(jnp.int32), (NE, width))
        picked = jnp.zeros((NE, width), F32)
        for x in range(nx):
            for z in range(nz):
                row = jnp.broadcast_to(xbuf[x, z], (NE, width))
                picked = jnp.where(owner_wide == x * nz + z, row, picked)
        s_lane = lax.broadcasted_iota(jnp.int32, (NE, width), 1)
        first = (cur * (width // (4 * n_cur)) + rank) * 4
        heat = []
        for c in range(4):
            surf = jnp.sum(jnp.where(s_lane == first + c, picked, 0.0), axis=1, keepdims=True)
            part = slice(NE * c, NE * c + NE)
            heat.append(
                0.2
                * (
                    downward[part]
                    + surf * upward[part]
                    - jnp.tanh(cols[0, pl.ds(NE * c, NE), :]) * emitted[part]
                )
            )
        return heat

    count = [1 + sum(p in edge for edge in EDGES) for p in range(16)]
    for v in SEND_ORDER:
        if v == 2:
            heat = heating()
        for step in range(2):
            if step == 1:
                rim_copies[0, v].wait()
                rim_copies[1, v].wait()
            for f in range(4):
                for m in range(4):
                    b = RIM.index(EDGES[f][3 - m])
                    lanes = pl.ds(NL * m, NL)
                    for s, ref in ((1, own),) if step == 0 else ((0, left), (2, right)):
                        high, low = split(ref[v, b])
                        rhs[pl.ds(192 * f + 32 * s, 32), lanes] = high
                        rhs[pl.ds(192 * f + 96 + 32 * s, 32), lanes] = low
        got = jnp.dot(onehot[...], rhs[...], preferred_element_type=F32)
        for p in range(16):
            if p in RIM:
                tend = own[v, RIM.index(p)]
            else:
                tend = inner[v, INNER.index(p)]
            for k in range(4):
                if p in EDGES[k]:
                    m = EDGES[k].index(p)
                    tend = tend + got[NE * k : NE * k + NE, NL * m : NL * m + NL]
            value = state[:, slab(p, v)] + tend * (0.2 / count[p])
            if v == 2:
                value = value + heat[2 * (p // 8) + (p % 4) // 2]
            out[:, slab(p, v)] = value


def per_device(nx, nz, state, neighbour, neighbour_edge, owner, surface, k_water, k_tracer):
    width = surface.shape[1]
    vmem = pl.BlockSpec(memory_space=pltpu.VMEM)
    anywhere = pl.BlockSpec(memory_space=pl.ANY)
    args = (state, neighbour.T, neighbour_edge.T, owner.T, surface, k_water, k_tracer)
    sem = pltpu.SemaphoreType.DMA
    return pl.pallas_call(
        functools.partial(kernel, nx, nz),
        out_shape=pltpu.VMEM(state.shape, F32),
        in_specs=[anywhere] * 7,
        out_specs=vmem,
        scratch_shapes=[
            *[pltpu.VMEM(arg.shape, arg.dtype) for arg in args],
            pltpu.VMEM((NV, 12, NE, NL), F32),
            pltpu.VMEM((NV, 12, NE, NL), F32),
            pltpu.VMEM((NV, 12, NE, NL), F32),
            pltpu.VMEM((NV, 4, NE, NL), F32),
            pltpu.VMEM((3, NL, NL), F32),
            pltpu.VMEM((4, NL, NL), F32),
            pltpu.VMEM((NL, NL, NL), F32),
            pltpu.VMEM((8 * NL, NL), F32),
            pltpu.VMEM((8 * NL, NL), F32),
            pltpu.VMEM((8 * NL, NL), F32),
            pltpu.VMEM((2, NL + 8, NL), F32),
            pltpu.VMEM((NL, 768), BF16),
            pltpu.VMEM((768, 512), BF16),
            pltpu.VMEM((nz, 1, width), F32),
            pltpu.VMEM((nx, nz, 1, width), F32),
            sem((2, NV)),
            sem((2, NV)),
            sem((max(nz - 1, 1),)),
            sem((max(nz - 1, 1),)),
            sem((max(nx - 1, 1),)),
            sem((max(nx - 1, 1),)),
            sem((2,)),
            sem((NE // 8,)),
            sem((6,)),
            *[pltpu.SemaphoreType.REGULAR] * 4,
        ],
        compiler_params=pltpu.CompilerParams(collective_id=0, has_side_effects=True),
        name="dynamics_physics",
    )(*args)


def solution(mesh):
    n_cur = mesh.shape["cur"]
    nx = 4 if n_cur % 4 == 0 and n_cur > 4 else 2
    nz = n_cur // nx
    both = P(("blk", "cur"), None)
    return jax.shard_map(
        functools.partial(per_device, nx, nz),
        mesh=mesh,
        in_specs=(both, both, both, both, both, P(), P()),
        out_specs=both,
        check_vma=False,
    )
```

```python
import functools
import math

import jax
import jax.numpy as jnp
import numpy as np
from jax import lax
from jax.experimental import pallas as pl
from jax.experimental.pallas import tpu as pltpu
from jax.sharding import PartitionSpec as P

MESH = pl.DeviceIdType.MESH
F32 = jnp.float32
BF16 = jnp.bfloat16
EDGES = ((0, 4, 8, 12), (12, 13, 14, 15), (15, 11, 7, 3), (3, 2, 1, 0))
RIM = (0, 1, 2, 3, 4, 7, 8, 11, 12, 13, 14, 15)
INNER = (5, 6, 9, 10)
SEND_ORDER = (0, 1, 3, 4, 2)
EARLY = 3
NE = 32
NV = 5
NL = 128


def gll_matrix():
    nodes = np.array([-1.0, -1.0 / np.sqrt(5.0), 1.0 / np.sqrt(5.0), 1.0])
    weights = np.array(
        [1.0 / np.prod([nodes[c] - nodes[o] for o in range(4) if o != c]) for c in range(4)]
    )
    matrix = np.zeros((4, 4))
    for r in range(4):
        for c in range(4):
            if r != c:
                matrix[r, c] = weights[c] / weights[r] / (nodes[r] - nodes[c])
        matrix[r, r] = -np.sum(matrix[r])
    return matrix


def weighted(terms):
    total = None
    for weight, value in terms:
        if abs(weight) < 1e-12:
            continue
        part = value * float(weight)
        total = part if total is None else total + part
    return total


def slab(p, v):
    return pl.ds((p * NV + v) * NL, NL)


def split(x):
    high = x.astype(BF16)
    low = (x - high.astype(F32)).astype(BF16)
    return high, low


def fold(x):
    rows = x.shape[0] // 8
    parts = [x[8 * i : 8 * i + 8] for i in range(rows)]
    while len(parts) > 1:
        parts = [parts[i] + parts[i + 1] for i in range(0, len(parts), 2)]
    return parts[0]


def kernel(
    nx,
    nz,
    state_in,
    nbr_in,
    nedge_in,
    owner_in,
    surface_in,
    kw_in,
    kt_in,
    out,
    state,
    nbr,
    nedge,
    owner,
    surface,
    kw,
    kt,
    own,
    left,
    right,
    inner,
    cols,
    wt,
    tran,
    st_part,
    sp_part,
    sq_part,
    shift,
    onehot,
    rhs,
    zbuf,
    xbuf,
    rim_send,
    rim_recv,
    z_send,
    z_recv,
    x_send,
    x_recv,
    copy_sem,
    row_sem,
    load_sem,
    z_near,
    z_mid,
    z_far,
    x_near,
):
    blk = lax.axis_index("blk")
    cur = lax.axis_index("cur")
    n_blk = lax.axis_size("blk")
    n_cur = nx * nz
    n_dev = n_blk * n_cur
    me = blk * n_cur + cur
    my_x = cur // nz
    my_z = cur % nz

    def place(index):
        return (index // n_cur, index % n_cur)

    after = place(lax.rem(me + 1, n_dev))
    before = place(lax.rem(me + n_dev - 1, n_dev))

    def z_peer(j):
        return (blk, my_x * nz + lax.rem(my_z + j + nz, nz))

    def x_peer(j):
        return (blk, lax.rem(my_x + j + nx, nx) * nz + my_z)

    def tell(sem, peer):
        pl.semaphore_signal(sem, inc=1, device_id=peer, device_id_type=MESH)

    barrier = pltpu.get_barrier_semaphore()
    peers = [after, before, z_peer(1), z_peer(-1), x_peer(1), x_peer(-1)]
    for peer in peers:
        tell(barrier, peer)
    loads = []
    rows_in = []
    for g in range(NE // 8):
        rows = pl.ds(8 * g, 8)
        load = pltpu.make_async_copy(state_in.at[rows, :], state.at[rows, :], row_sem.at[g])
        load.start()
        rows_in.append(load)
    pairs = (
        (surface_in, surface),
        (kw_in, kw),
        (kt_in, kt),
        (nbr_in, nbr),
        (nedge_in, nedge),
        (owner_in, owner),
    )
    for i, (src, dst) in enumerate(pairs):
        load = pltpu.make_async_copy(src, dst, load_sem.at[i])
        load.start()
        loads.append(load)

    d_matrix = -0.5 * gll_matrix()

    def tend_rows(v, g, _):
        rows = pl.ds(pl.multiple_of(8 * g, 8), 8)
        q = [state[rows, slab(p, v)] for p in range(16)]
        for i in range(4):
            for j in range(4):
                p = 4 * i + j
                qx = weighted([(d_matrix[i, a], q[4 * a + j]) for a in range(4)])
                qy = weighted([(d_matrix[j, b], q[4 * i + b]) for b in range(4)])
                tend = state[rows, slab(p, 0)] * qx + state[rows, slab(p, 1)] * qy
                if p in RIM:
                    own[v, RIM.index(p), rows, :] = tend
                else:
                    inner[v, INNER.index(p), rows, :] = tend
        return 0

    def tend_of(v):
        lax.fori_loop(0, NE // 8, functools.partial(tend_rows, v), 0)

    rim_copies = {}

    def send_rim(v):
        for side, (dst, peer) in enumerate(((left, after), (right, before))):
            copy = pltpu.make_async_remote_copy(
                src_ref=own.at[v],
                dst_ref=dst.at[v],
                send_sem=rim_send.at[side, v],
                recv_sem=rim_recv.at[side, v],
                device_id=peer,
                device_id_type=MESH,
            )
            copy.start()
            rim_copies[side, v] = copy

    for g in range(NE // 8):
        rows_in[g].wait()
        tend_rows(SEND_ORDER[0], g, 0)
    pl.semaphore_wait(barrier, len(peers))
    tell(z_near, z_peer(1))
    tell(z_near, z_peer(-1))
    tell(x_near, x_peer(1))
    tell(x_near, x_peer(-1))
    send_rim(SEND_ORDER[0])
    for load in loads:
        load.wait()
    keep = pltpu.make_async_copy(surface, xbuf.at[my_x], copy_sem.at[0])
    keep.start()
    x_copies = []

    def send_x(j):
        copy = pltpu.make_async_remote_copy(
            src_ref=surface,
            dst_ref=xbuf.at[my_x],
            send_sem=x_send.at[j - 1],
            recv_sem=x_recv.at[j - 1],
            device_id=x_peer(j),
            device_id_type=MESH,
        )
        copy.start()
        x_copies.append(copy)

    for j in sorted({1, nx - 1}):
        send_x(j)
    for v in SEND_ORDER[1:EARLY]:
        tend_of(v)
        send_rim(v)
    pl.semaphore_wait(x_near, 2)
    for j in range(2, nx - 1):
        send_x(j)
    pl.semaphore_wait(z_near, 2)
    tell(z_mid, z_peer(2))
    tell(z_mid, z_peer(-2))
    for v in SEND_ORDER[EARLY:]:
        tend_of(v)

    quad = (1.0 / 6.0, 5.0 / 6.0, 5.0 / 6.0, 1.0 / 6.0)
    for c in range(4):
        points = [4 * i + j for i in range(4) for j in range(4) if 2 * (i // 2) + j // 2 == c]
        for r in range(3):
            value = weighted(
                [(quad[p // 4] * quad[p % 4], state[:, slab(p, 2 + r)]) for p in points]
            )
            if r > 0:
                value = jnp.maximum(value, 0.0) + jnp.log1p(jnp.exp(-jnp.abs(value)))
            cols[r, pl.ds(NE * c, NE), :] = value
    for r in range(2):
        turned = cols[r + 1].T
        high = turned.astype(BF16).astype(F32)
        wt[2 * r] = high
        wt[2 * r + 1] = turned - high

    row_in_16 = lax.broadcasted_iota(jnp.int32, (128, NL), 0) % 16
    scale = -math.log2(math.e)

    def depth_group(group, _):
        rows = pl.ds(pl.multiple_of(16 * group, 16), 16)
        kw_f = kw[rows, :] * scale
        kt_f = kt[rows, :] * scale
        kw_h = kw_f.astype(BF16).astype(F32)
        kt_h = kt_f.astype(BF16).astype(F32)
        zero = jnp.zeros((32, NL), F32)
        k_stack = jnp.concatenate(
            [kw_h, kw_h, kw_f - kw_h, kt_h, kt_h, kt_f - kt_h, zero], axis=0
        )
        k_turned = k_stack.T.astype(BF16)
        w_h, w_l, t_h, t_l = (wt[i, rows, :] for i in range(4))
        w_stack = jnp.concatenate([w_h, w_l, w_h, t_h, t_l, t_h, zero], axis=0)
        for i in range(16):
            one = jnp.where(row_in_16 == i, w_stack, 0.0).astype(BF16)
            power = jnp.dot(k_turned, one, preferred_element_type=F32)
            passed = jnp.exp2(power)
            level = 16 * group + i
            tran[level] = passed
            st_part[pl.ds(pl.multiple_of(8 * level, 8), 8), :] = fold(passed)
        return 0

    half = NL // 32
    pl.semaphore_wait(z_mid, 2)
    tell(z_far, z_peer(2))
    tell(z_far, z_peer(-2))
    lax.fori_loop(0, half, depth_group, 0)
    keep.wait()
    for copy in x_copies:
        copy.wait()
    per = surface.shape[1] // n_cur

    def window(z):
        first = (my_x * nz + z) * per // NL * NL
        return xbuf.at[:, :, pl.ds(pl.multiple_of(first, NL), NL)]

    keep_z = pltpu.make_async_copy(window(my_z), zbuf.at[my_z], copy_sem.at[1])
    keep_z.start()
    pl.semaphore_wait(z_far, 2)
    z_copies = []
    for j in range(1, nz):
        copy = pltpu.make_async_remote_copy(
            src_ref=window(lax.rem(my_z + j, nz)),
            dst_ref=zbuf.at[my_z],
            send_sem=z_send.at[j - 1],
            recv_sem=z_recv.at[j - 1],
            device_id=z_peer(j),
            device_id_type=MESH,
        )
        copy.start()
        z_copies.append(copy)
    for v in SEND_ORDER[EARLY:]:
        send_rim(v)
    lax.fori_loop(half, 2 * half, depth_group, 0)

    def march(level, carry):
        down, up = carry
        back = NL - 1 - level
        down = down * tran[level]
        sp_part[pl.ds(pl.multiple_of(8 * level, 8), 8), :] = fold(down)
        sq_part[pl.ds(pl.multiple_of(8 * back, 8), 8), :] = fold(up)
        up = up * tran[back]
        return down, up

    ones = jnp.ones((NL, NL), F32)
    lax.fori_loop(0, NL, march, (ones, ones))

    def total(part):
        return sum(part[pl.ds(s, NL, stride=8), :] for s in range(8))

    sum_t, sum_p, sum_q = total(st_part), total(sp_part), total(sq_part)
    shift[0, pl.ds(0, 8), :] = jnp.full((8, NL), float(NL), F32)
    shift[0, pl.ds(8, NL), :] = sum_p
    shift[1, pl.ds(0, 8), :] = jnp.broadcast_to(sum_p[NL - 1 : NL], (8, NL))
    shift[1, pl.ds(8, NL), :] = sum_q
    inv = 1.0 / NL
    downward = ((shift[0, pl.ds(7, NL), :] - sum_p) * (64.0 * inv)).T
    upward = ((sum_q - shift[1, pl.ds(7, NL), :]) * (2.0 * inv)).T
    emitted = (8.0 - sum_t * (8.0 * inv)).T

    base = me * NE - NE
    elems = n_dev * NE
    local = nbr[...] - base
    local = jnp.where(local < 0, local + elems, local)
    local = jnp.where(local >= elems, local - elems, local)
    target = nedge[...] * 192 + local
    lane = lax.broadcasted_iota(jnp.int32, (NE, 768), 1)
    sub = lax.broadcasted_iota(jnp.int32, (NE, NE), 0)
    lan = lax.broadcasted_iota(jnp.int32, (NE, NE), 1)

    def column(row):
        return jnp.sum(jnp.where(sub == lan, row, 0.0), axis=1, keepdims=True)

    for k in range(4):
        row = jnp.broadcast_to(target[k : k + 1, :].astype(F32), (NE, NE))
        want = column(row).astype(jnp.int32)
        hit = (lane == want) | (lane == want + 96)
        onehot[pl.ds(NE * k, NE), :] = hit.astype(F32).astype(BF16)

    own_row = jnp.broadcast_to(owner[...].astype(F32), (NE, NE))
    own_col = column(own_row)
    earlier = (own_col == own_row) & (lan < sub)
    rank = jnp.sum(jnp.where(earlier, 1.0, 0.0), axis=1, keepdims=True).astype(jnp.int32)

    def heating():
        keep_z.wait()
        for copy in z_copies:
            copy.wait()
        owner_wide = jnp.broadcast_to(own_col.astype(jnp.int32), (NE, NL))
        picked = jnp.zeros((NE, NL), F32)
        for x in range(nx):
            for z in range(nz):
                row = jnp.broadcast_to(zbuf[z, x], (NE, NL))
                picked = jnp.where(owner_wide == x * nz + z, row, picked)
        s_lane = lax.broadcasted_iota(jnp.int32, (NE, NL), 1)
        first = lax.rem(cur * per, NL) + rank * 4
        heat = []
        for c in range(4):
            surf = jnp.sum(jnp.where(s_lane == first + c, picked, 0.0), axis=1, keepdims=True)
            part = slice(NE * c, NE * c + NE)
            heat.append(
                0.2
                * (
                    downward[part]
                    + surf * upward[part]
                    - jnp.tanh(cols[0, pl.ds(NE * c, NE), :]) * emitted[part]
                )
            )
        return heat

    count = [1 + sum(p in edge for edge in EDGES) for p in range(16)]
    for v in SEND_ORDER:
        if v == 2:
            heat = heating()
        for step in range(2):
            if step == 1:
                rim_copies[0, v].wait()
                rim_copies[1, v].wait()
            for f in range(4):
                for m in range(4):
                    b = RIM.index(EDGES[f][3 - m])
                    lanes = pl.ds(NL * m, NL)
                    for s, ref in ((1, own),) if step == 0 else ((0, left), (2, right)):
                        high, low = split(ref[v, b])
                        rhs[pl.ds(192 * f + 32 * s, 32), lanes] = high
                        rhs[pl.ds(192 * f + 96 + 32 * s, 32), lanes] = low
        got = jnp.dot(onehot[...], rhs[...], preferred_element_type=F32)
        for p in range(16):
            if p in RIM:
                tend = own[v, RIM.index(p)]
            else:
                tend = inner[v, INNER.index(p)]
            for k in range(4):
                if p in EDGES[k]:
                    m = EDGES[k].index(p)
                    tend = tend + got[NE * k : NE * k + NE, NL * m : NL * m + NL]
            value = state[:, slab(p, v)] + tend * (0.2 / count[p])
            if v == 2:
                value = value + heat[2 * (p // 8) + (p % 4) // 2]
            out[:, slab(p, v)] = value


def per_device(nx, nz, state, neighbour, neighbour_edge, owner, surface, k_water, k_tracer):
    width = surface.shape[1]
    vmem = pl.BlockSpec(memory_space=pltpu.VMEM)
    anywhere = pl.BlockSpec(memory_space=pl.ANY)
    args = (state, neighbour.T, neighbour_edge.T, owner.T, surface, k_water, k_tracer)
    sem = pltpu.SemaphoreType.DMA
    return pl.pallas_call(
        functools.partial(kernel, nx, nz),
        out_shape=pltpu.VMEM(state.shape, F32),
        in_specs=[anywhere] * 7,
        out_specs=vmem,
        scratch_shapes=[
            *[pltpu.VMEM(arg.shape, arg.dtype) for arg in args],
            pltpu.VMEM((NV, 12, NE, NL), F32),
            pltpu.VMEM((NV, 12, NE, NL), F32),
            pltpu.VMEM((NV, 12, NE, NL), F32),
            pltpu.VMEM((NV, 4, NE, NL), F32),
            pltpu.VMEM((3, NL, NL), F32),
            pltpu.VMEM((4, NL, NL), F32),
            pltpu.VMEM((NL, NL, NL), F32),
            pltpu.VMEM((8 * NL, NL), F32),
            pltpu.VMEM((8 * NL, NL), F32),
            pltpu.VMEM((8 * NL, NL), F32),
            pltpu.VMEM((2, NL + 8, NL), F32),
            pltpu.VMEM((NL, 768), BF16),
            pltpu.VMEM((768, 512), BF16),
            pltpu.VMEM((nz, nx, 1, NL), F32),
            pltpu.VMEM((nx, 1, width), F32),
            sem((2, NV)),
            sem((2, NV)),
            sem((max(nz - 1, 1),)),
            sem((max(nz - 1, 1),)),
            sem((max(nx - 1, 1),)),
            sem((max(nx - 1, 1),)),
            sem((2,)),
            sem((NE // 8,)),
            sem((6,)),
            *[pltpu.SemaphoreType.REGULAR] * 4,
        ],
        compiler_params=pltpu.CompilerParams(collective_id=0, has_side_effects=True),
        name="dynamics_physics",
    )(*args)


def solution(mesh):
    n_cur = mesh.shape["cur"]
    nx = 4 if n_cur % 4 == 0 and n_cur > 4 else 2
    nz = n_cur // nx
    both = P(("blk", "cur"), None)
    return jax.shard_map(
        functools.partial(per_device, nx, nz),
        mesh=mesh,
        in_specs=(both, both, both, both, both, P(), P()),
        out_specs=both,
        check_vma=False,
    )
```

```python
import functools
import math

import jax
import jax.numpy as jnp
import numpy as np
from jax import lax
from jax.experimental import pallas as pl
from jax.experimental.pallas import tpu as pltpu
from jax.sharding import PartitionSpec as P

MESH = pl.DeviceIdType.MESH
F32 = jnp.float32
BF16 = jnp.bfloat16
EDGES = ((0, 4, 8, 12), (12, 13, 14, 15), (15, 11, 7, 3), (3, 2, 1, 0))
RIM = (0, 1, 2, 3, 4, 7, 8, 11, 12, 13, 14, 15)
INNER = (5, 6, 9, 10)
SEND_ORDER = (0, 1, 3, 4, 2)
EARLY = 3
NE = 32
NV = 5
NL = 128


def gll_matrix():
    nodes = np.array([-1.0, -1.0 / np.sqrt(5.0), 1.0 / np.sqrt(5.0), 1.0])
    weights = np.array(
        [1.0 / np.prod([nodes[c] - nodes[o] for o in range(4) if o != c]) for c in range(4)]
    )
    matrix = np.zeros((4, 4))
    for r in range(4):
        for c in range(4):
            if r != c:
                matrix[r, c] = weights[c] / weights[r] / (nodes[r] - nodes[c])
        matrix[r, r] = -np.sum(matrix[r])
    return matrix


def weighted(terms):
    total = None
    for weight, value in terms:
        if abs(weight) < 1e-12:
            continue
        part = value * float(weight)
        total = part if total is None else total + part
    return total


def slab(p, v):
    return pl.ds((p * NV + v) * NL, NL)


def split(x):
    high = x.astype(BF16)
    low = (x - high.astype(F32)).astype(BF16)
    return high, low


def fold(x):
    rows = x.shape[0] // 8
    parts = [x[8 * i : 8 * i + 8] for i in range(rows)]
    while len(parts) > 1:
        parts = [parts[i] + parts[i + 1] for i in range(0, len(parts), 2)]
    return parts[0]


def kernel(
    nx,
    nz,
    state_in,
    nbr_in,
    nedge_in,
    owner_in,
    surface_in,
    kw_in,
    kt_in,
    out,
    state,
    nbr,
    nedge,
    owner,
    surface,
    kw,
    kt,
    own,
    left,
    right,
    inner,
    cols,
    wt,
    tran,
    st_part,
    sp_part,
    sq_part,
    shift,
    onehot,
    rhs,
    zbuf,
    xbuf,
    rim_send,
    rim_recv,
    z_send,
    z_recv,
    x_send,
    x_recv,
    copy_sem,
    row_sem,
    load_sem,
    z_near,
    z_mid,
    z_far,
    x_near,
):
    blk = lax.axis_index("blk")
    cur = lax.axis_index("cur")
    n_blk = lax.axis_size("blk")
    n_cur = nx * nz
    n_dev = n_blk * n_cur
    me = blk * n_cur + cur
    my_x = cur // nz
    my_z = cur % nz

    def place(index):
        return (index // n_cur, index % n_cur)

    after = place(lax.rem(me + 1, n_dev))
    before = place(lax.rem(me + n_dev - 1, n_dev))

    def z_peer(j):
        return (blk, my_x * nz + lax.rem(my_z + j + nz, nz))

    def x_peer(j):
        return (blk, lax.rem(my_x + j + nx, nx) * nz + my_z)

    def tell(sem, peer):
        pl.semaphore_signal(sem, inc=1, device_id=peer, device_id_type=MESH)

    barrier = pltpu.get_barrier_semaphore()
    peers = [after, before, z_peer(1), z_peer(-1), x_peer(1), x_peer(-1)]
    for peer in peers:
        tell(barrier, peer)
    loads = []
    rows_in = []
    for part, (start, size) in enumerate(((0, 2 * NL), (2 * NL, 3 * NL))):
        for p in range(16):
            lanes = pl.ds(p * NV * NL + start, size)
            load = pltpu.make_async_copy(
                state_in.at[:, lanes], state.at[:, lanes], row_sem.at[part, p]
            )
            load.start()
            rows_in.append(load)
    pairs = (
        (surface_in, surface),
        (kw_in, kw),
        (kt_in, kt),
        (nbr_in, nbr),
        (nedge_in, nedge),
        (owner_in, owner),
    )
    for i, (src, dst) in enumerate(pairs):
        load = pltpu.make_async_copy(src, dst, load_sem.at[i])
        load.start()
        loads.append(load)

    d_matrix = -0.5 * gll_matrix()

    def tend_rows(v, g, _):
        rows = pl.ds(pl.multiple_of(8 * g, 8), 8)
        q = [state[rows, slab(p, v)] for p in range(16)]
        for i in range(4):
            for j in range(4):
                p = 4 * i + j
                qx = weighted([(d_matrix[i, a], q[4 * a + j]) for a in range(4)])
                qy = weighted([(d_matrix[j, b], q[4 * i + b]) for b in range(4)])
                tend = state[rows, slab(p, 0)] * qx + state[rows, slab(p, 1)] * qy
                if p in RIM:
                    own[v, RIM.index(p), rows, :] = tend
                else:
                    inner[v, INNER.index(p), rows, :] = tend
        return 0

    def tend_of(v):
        lax.fori_loop(0, NE // 8, functools.partial(tend_rows, v), 0)

    rim_copies = {}

    def send_rim(v):
        for side, (dst, peer) in enumerate(((left, after), (right, before))):
            copy = pltpu.make_async_remote_copy(
                src_ref=own.at[v],
                dst_ref=dst.at[v],
                send_sem=rim_send.at[side, v],
                recv_sem=rim_recv.at[side, v],
                device_id=peer,
                device_id_type=MESH,
            )
            copy.start()
            rim_copies[side, v] = copy

    for load in rows_in[:16]:
        load.wait()
    tend_of(SEND_ORDER[0])
    pl.semaphore_wait(barrier, len(peers))
    tell(z_near, z_peer(1))
    tell(z_near, z_peer(-1))
    tell(x_near, x_peer(1))
    tell(x_near, x_peer(-1))
    send_rim(SEND_ORDER[0])
    for load in loads + rows_in[16:]:
        load.wait()
    keep = pltpu.make_async_copy(surface, xbuf.at[my_x], copy_sem.at[0])
    keep.start()
    x_copies = []

    def send_x(j):
        copy = pltpu.make_async_remote_copy(
            src_ref=surface,
            dst_ref=xbuf.at[my_x],
            send_sem=x_send.at[j - 1],
            recv_sem=x_recv.at[j - 1],
            device_id=x_peer(j),
            device_id_type=MESH,
        )
        copy.start()
        x_copies.append(copy)

    for j in sorted({1, nx - 1}):
        send_x(j)
    for v in SEND_ORDER[1:EARLY]:
        tend_of(v)
        send_rim(v)
    pl.semaphore_wait(x_near, 2)
    for j in range(2, nx - 1):
        send_x(j)
    pl.semaphore_wait(z_near, 2)
    tell(z_mid, z_peer(2))
    tell(z_mid, z_peer(-2))
    for v in SEND_ORDER[EARLY:]:
        tend_of(v)

    quad = (1.0 / 6.0, 5.0 / 6.0, 5.0 / 6.0, 1.0 / 6.0)
    for c in range(4):
        points = [4 * i + j for i in range(4) for j in range(4) if 2 * (i // 2) + j // 2 == c]
        for r in range(3):
            value = weighted(
                [(quad[p // 4] * quad[p % 4], state[:, slab(p, 2 + r)]) for p in points]
            )
            if r > 0:
                value = jnp.maximum(value, 0.0) + jnp.log1p(jnp.exp(-jnp.abs(value)))
            cols[r, pl.ds(NE * c, NE), :] = value
    for r in range(2):
        turned = cols[r + 1].T
        high = turned.astype(BF16).astype(F32)
        wt[2 * r] = high
        wt[2 * r + 1] = turned - high

    row_in_16 = lax.broadcasted_iota(jnp.int32, (128, NL), 0) % 16
    scale = -math.log2(math.e)

    def depth_group(group, _):
        rows = pl.ds(pl.multiple_of(16 * group, 16), 16)
        kw_f = kw[rows, :] * scale
        kt_f = kt[rows, :] * scale
        kw_h = kw_f.astype(BF16).astype(F32)
        kt_h = kt_f.astype(BF16).astype(F32)
        zero = jnp.zeros((32, NL), F32)
        k_stack = jnp.concatenate(
            [kw_h, kw_h, kw_f - kw_h, kt_h, kt_h, kt_f - kt_h, zero], axis=0
        )
        k_turned = k_stack.T.astype(BF16)
        w_h, w_l, t_h, t_l = (wt[i, rows, :] for i in range(4))
        w_stack = jnp.concatenate([w_h, w_l, w_h, t_h, t_l, t_h, zero], axis=0)
        for i in range(16):
            one = jnp.where(row_in_16 == i, w_stack, 0.0).astype(BF16)
            power = jnp.dot(k_turned, one, preferred_element_type=F32)
            passed = jnp.exp2(power)
            level = 16 * group + i
            tran[level] = passed
            st_part[pl.ds(pl.multiple_of(8 * level, 8), 8), :] = fold(passed)
        return 0

    half = NL // 32
    pl.semaphore_wait(z_mid, 2)
    tell(z_far, z_peer(2))
    tell(z_far, z_peer(-2))
    lax.fori_loop(0, half, depth_group, 0)
    keep.wait()
    for copy in x_copies:
        copy.wait()
    per = surface.shape[1] // n_cur

    def window(z):
        first = (my_x * nz + z) * per // NL * NL
        return xbuf.at[:, :, pl.ds(pl.multiple_of(first, NL), NL)]

    keep_z = pltpu.make_async_copy(window(my_z), zbuf.at[my_z], copy_sem.at[1])
    keep_z.start()
    pl.semaphore_wait(z_far, 2)
    z_copies = []
    for j in range(1, nz):
        copy = pltpu.make_async_remote_copy(
            src_ref=window(lax.rem(my_z + j, nz)),
            dst_ref=zbuf.at[my_z],
            send_sem=z_send.at[j - 1],
            recv_sem=z_recv.at[j - 1],
            device_id=z_peer(j),
            device_id_type=MESH,
        )
        copy.start()
        z_copies.append(copy)
    for v in SEND_ORDER[EARLY:]:
        send_rim(v)
    lax.fori_loop(half, 2 * half, depth_group, 0)

    def march(level, carry):
        down, up = carry
        back = NL - 1 - level
        down = down * tran[level]
        sp_part[pl.ds(pl.multiple_of(8 * level, 8), 8), :] = fold(down)
        sq_part[pl.ds(pl.multiple_of(8 * back, 8), 8), :] = fold(up)
        up = up * tran[back]
        return down, up

    ones = jnp.ones((NL, NL), F32)
    lax.fori_loop(0, NL, march, (ones, ones))

    def total(part):
        return sum(part[pl.ds(s, NL, stride=8), :] for s in range(8))

    sum_t, sum_p, sum_q = total(st_part), total(sp_part), total(sq_part)
    shift[0, pl.ds(0, 8), :] = jnp.full((8, NL), float(NL), F32)
    shift[0, pl.ds(8, NL), :] = sum_p
    shift[1, pl.ds(0, 8), :] = jnp.broadcast_to(sum_p[NL - 1 : NL], (8, NL))
    shift[1, pl.ds(8, NL), :] = sum_q
    inv = 1.0 / NL
    downward = ((shift[0, pl.ds(7, NL), :] - sum_p) * (64.0 * inv)).T
    upward = ((sum_q - shift[1, pl.ds(7, NL), :]) * (2.0 * inv)).T
    emitted = (8.0 - sum_t * (8.0 * inv)).T

    base = me * NE - NE
    elems = n_dev * NE
    local = nbr[...] - base
    local = jnp.where(local < 0, local + elems, local)
    local = jnp.where(local >= elems, local - elems, local)
    target = nedge[...] * 192 + local
    lane = lax.broadcasted_iota(jnp.int32, (NE, 768), 1)
    sub = lax.broadcasted_iota(jnp.int32, (NE, NE), 0)
    lan = lax.broadcasted_iota(jnp.int32, (NE, NE), 1)

    def column(row):
        return jnp.sum(jnp.where(sub == lan, row, 0.0), axis=1, keepdims=True)

    for k in range(4):
        row = jnp.broadcast_to(target[k : k + 1, :].astype(F32), (NE, NE))
        want = column(row).astype(jnp.int32)
        hit = (lane == want) | (lane == want + 96)
        onehot[pl.ds(NE * k, NE), :] = hit.astype(F32).astype(BF16)

    own_row = jnp.broadcast_to(owner[...].astype(F32), (NE, NE))
    own_col = column(own_row)
    earlier = (own_col == own_row) & (lan < sub)
    rank = jnp.sum(jnp.where(earlier, 1.0, 0.0), axis=1, keepdims=True).astype(jnp.int32)

    def heating():
        keep_z.wait()
        for copy in z_copies:
            copy.wait()
        owner_wide = jnp.broadcast_to(own_col.astype(jnp.int32), (NE, NL))
        picked = jnp.zeros((NE, NL), F32)
        for x in range(nx):
            for z in range(nz):
                row = jnp.broadcast_to(zbuf[z, x], (NE, NL))
                picked = jnp.where(owner_wide == x * nz + z, row, picked)
        s_lane = lax.broadcasted_iota(jnp.int32, (NE, NL), 1)
        first = lax.rem(cur * per, NL) + rank * 4
        heat = []
        for c in range(4):
            surf = jnp.sum(jnp.where(s_lane == first + c, picked, 0.0), axis=1, keepdims=True)
            part = slice(NE * c, NE * c + NE)
            heat.append(
                0.2
                * (
                    downward[part]
                    + surf * upward[part]
                    - jnp.tanh(cols[0, pl.ds(NE * c, NE), :]) * emitted[part]
                )
            )
        return heat

    count = [1 + sum(p in edge for edge in EDGES) for p in range(16)]
    for v in SEND_ORDER:
        if v == 2:
            heat = heating()
        for step in range(2):
            if step == 1:
                rim_copies[0, v].wait()
                rim_copies[1, v].wait()
            for b in range(12):
                spots = [
                    (f, m) for f in range(4) for m in range(4) if EDGES[f][3 - m] == RIM[b]
                ]
                for s, ref in ((1, own),) if step == 0 else ((0, left), (2, right)):
                    high, low = split(ref[v, b])
                    for f, m in spots:
                        lanes = pl.ds(NL * m, NL)
                        rhs[pl.ds(192 * f + 32 * s, 32), lanes] = high
                        rhs[pl.ds(192 * f + 96 + 32 * s, 32), lanes] = low
        got = jnp.dot(onehot[...], rhs[...], preferred_element_type=F32)
        for p in range(16):
            if p in RIM:
                tend = own[v, RIM.index(p)]
            else:
                tend = inner[v, INNER.index(p)]
            for k in range(4):
                if p in EDGES[k]:
                    m = EDGES[k].index(p)
                    tend = tend + got[NE * k : NE * k + NE, NL * m : NL * m + NL]
            value = state[:, slab(p, v)] + tend * (0.2 / count[p])
            if v == 2:
                value = value + heat[2 * (p // 8) + (p % 4) // 2]
            out[:, slab(p, v)] = value


def per_device(nx, nz, state, neighbour, neighbour_edge, owner, surface, k_water, k_tracer):
    width = surface.shape[1]
    vmem = pl.BlockSpec(memory_space=pltpu.VMEM)
    anywhere = pl.BlockSpec(memory_space=pl.ANY)
    args = (state, neighbour.T, neighbour_edge.T, owner.T, surface, k_water, k_tracer)
    sem = pltpu.SemaphoreType.DMA
    return pl.pallas_call(
        functools.partial(kernel, nx, nz),
        out_shape=pltpu.VMEM(state.shape, F32),
        in_specs=[anywhere] * 7,
        out_specs=vmem,
        scratch_shapes=[
            *[pltpu.VMEM(arg.shape, arg.dtype) for arg in args],
            pltpu.VMEM((NV, 12, NE, NL), F32),
            pltpu.VMEM((NV, 12, NE, NL), F32),
            pltpu.VMEM((NV, 12, NE, NL), F32),
            pltpu.VMEM((NV, 4, NE, NL), F32),
            pltpu.VMEM((3, NL, NL), F32),
            pltpu.VMEM((4, NL, NL), F32),
            pltpu.VMEM((NL, NL, NL), F32),
            pltpu.VMEM((8 * NL, NL), F32),
            pltpu.VMEM((8 * NL, NL), F32),
            pltpu.VMEM((8 * NL, NL), F32),
            pltpu.VMEM((2, NL + 8, NL), F32),
            pltpu.VMEM((NL, 768), BF16),
            pltpu.VMEM((768, 512), BF16),
            pltpu.VMEM((nz, nx, 1, NL), F32),
            pltpu.VMEM((nx, 1, width), F32),
            sem((2, NV)),
            sem((2, NV)),
            sem((max(nz - 1, 1),)),
            sem((max(nz - 1, 1),)),
            sem((max(nx - 1, 1),)),
            sem((max(nx - 1, 1),)),
            sem((2,)),
            sem((2, 16)),
            sem((6,)),
            *[pltpu.SemaphoreType.REGULAR] * 4,
        ],
        compiler_params=pltpu.CompilerParams(collective_id=0, has_side_effects=True),
        name="dynamics_physics",
    )(*args)


def solution(mesh):
    n_cur = mesh.shape["cur"]
    nx = 4 if n_cur % 4 == 0 and n_cur > 4 else 2
    nz = n_cur // nx
    both = P(("blk", "cur"), None)
    return jax.shard_map(
        functools.partial(per_device, nx, nz),
        mesh=mesh,
        in_specs=(both, both, both, both, both, P(), P()),
        out_specs=both,
        check_vma=False,
    )
```
